32 devices in a mesh: rows: 16 (over z, y, x), chip: 2 (over core).
Axes of the slice: x: 2, y: 2, z: 4, core: 2. Of those that a mesh axis runs over, the one named last changes fastest.
Arguments:
- hamiltonian: float32 [24576, 24576], P(('rows', 'chip')), may hold values from -1 to 4, as said below
- vectors: float32 [24576, 256], P(('rows', 'chip')), may hold values from -6 to 6
Outputs:
- ritz_block: float32 [24576, 256], P(('rows', 'chip'))
- projected: float32 [256, 256], replicated
The draws below stay inside these ranges and needn't reach their ends.
Inputs may be any that keep to these rules, and one draw needn't show every extreme that they name: hamiltonian is symmetric and positive definite.
All inputs are finite; a program needn't handle non-finite values.
Results may differ from the reference program's by a relative error of at most 0.003.
Values may be sent and summed in bfloat16 or wider, within the bound.
No kernel may reach another device: no remote copies, remote signals or barrier semaphores. Data moves between devices by JAX's collectives and lax.ppermute only.
A program may use at most 128 MiB of HBM per device.

```python
import jax
import jax.numpy as jnp
from jax import lax

NORDER = 24576
NVEC = 256


def draw_hamiltonian(key, part):
    key_entries = jax.random.fold_in(key, 11)
    key_levels = jax.random.fold_in(key, 23)
    entries = jnp.clip(jax.random.normal(key_entries, (NORDER, NORDER), jnp.float32), -6.0, 6.0)
    levels = jax.random.uniform(key_levels, (NORDER,), jnp.float32, 1.5, 3.5)
    scale_entry = 0.35 / jnp.sqrt(jnp.float32(NORDER))
    coupled = (entries + entries.T) * scale_entry
    places = jnp.arange(NORDER, dtype=jnp.int32)
    coupled = coupled.at[places, places].add(levels)
    return coupled.astype(jnp.float32)


def shard_levels(key, dims, cuts, least, largest):
    def one(axis_at, blocks):
        steps = jax.random.uniform(jax.random.fold_in(jax.random.fold_in(key, 6), axis_at), (blocks,), jnp.float32, least / len(cuts), largest / len(cuts))
        return jnp.repeat(jnp.exp(steps), dims[axis_at] // blocks).reshape((-1,) + (1,) * (len(dims) - axis_at - 1))

    gain = one(*cuts[0])
    for cut in cuts[1:]:
        gain = gain * one(*cut)
    return gain


def bell_draw(rng, extent, scale, reach, pieces=(), kind=jnp.bfloat16):
    array = scale * jax.random.normal(rng, extent, jnp.float32)
    if pieces:
        array = array * shard_levels(rng, extent, pieces, -0.22, 0.18)
    return jnp.clip(array, -reach, reach).astype(kind)


def setup_inputs(seed: int = 0) -> dict:
    streams_of = jax.random.split(jax.random.key(seed), 3)
    hamiltonian = draw_hamiltonian(jax.random.fold_in(streams_of[2], 71), 0)
    vectors = bell_draw(streams_of[1], (NORDER, NVEC), 1.0, 6.0, ((0, 32),), jnp.float32)
    return {"hamiltonian": hamiltonian, "vectors": vectors}


def reference(hamiltonian, vectors):
    highest = lax.Precision.HIGHEST
    basis = vectors.astype(jnp.bfloat16)
    widened = basis.astype(jnp.float32)
    product = jnp.dot(hamiltonian, widened, precision=highest)
    correlation = jnp.dot(basis.T.astype(jnp.float32), basis.astype(jnp.float32), preferred_element_type=jnp.float32)
    coupling = jnp.dot(widened.T, product, precision=highest)
    gram = jnp.dot(product.T, product, precision=highest)
    symmetric = 0.5 * (coupling + coupling.T)
    lower = jnp.linalg.cholesky(correlation)
    half = lax.linalg.triangular_solve(lower, symmetric, left_side=True, lower=True)
    projected = lax.linalg.triangular_solve(lower, half.T, left_side=True, lower=True)
    factor = jnp.linalg.cholesky(gram)
    rotated = lax.linalg.triangular_solve(factor, product.T, left_side=True, lower=True)
    ritz_block = rotated.T * jnp.sqrt(jnp.float32(NORDER))
    return (ritz_block, projected)
```

```python
import jax
import jax.numpy as jnp
from jax import lax
from jax.experimental import pallas as pl
from jax.experimental.pallas import tpu as pltpu
from jax.sharding import PartitionSpec as P

AXES = ("rows", "chip")
F32 = jnp.float32
BF16 = jnp.bfloat16
NN = (((1,), (0,)), ((), ()))
NT = (((1,), (1,)), ((), ()))


def shards_plain(hamiltonian, vectors):
    highest = lax.Precision.HIGHEST
    basis = vectors.astype(BF16)
    widened = basis.astype(F32)
    correlation_part = jnp.dot(basis.T, basis, preferred_element_type=F32)
    whole = lax.all_gather(basis, AXES, axis=0, tiled=True)
    product = jnp.dot(hamiltonian, whole.astype(F32), precision=highest)
    coupling_part = jnp.dot(widened.T, product, precision=highest)
    gram_part = jnp.dot(product.T, product, precision=highest)
    correlation, coupling, gram = lax.psum((correlation_part, coupling_part, gram_part), AXES)
    symmetric = 0.5 * (coupling + coupling.T)
    lower = jnp.linalg.cholesky(correlation)
    half = lax.linalg.triangular_solve(lower, symmetric, left_side=True, lower=True)
    projected = lax.linalg.triangular_solve(lower, half.T, left_side=True, lower=True)
    factor = jnp.linalg.cholesky(gram)
    rotated = lax.linalg.triangular_solve(factor, product.T, left_side=True, lower=True)
    return (rotated.T * jnp.sqrt(F32(hamiltonian.shape[1])), projected)


def split(a):
    high = a.astype(BF16)
    return high, (a - high.astype(F32)).astype(BF16)


def dot1(a, b, dims=NN):
    return lax.dot_general(a, b, dims, preferred_element_type=F32)


def dot3(a, b, dims=NN):
    ah, al = split(a)
    bh, bl = split(b)
    return dot1(ah, bh, dims) + (dot1(ah, bl, dims) + dot1(al, bh, dims))


def stage_call(hamiltonian, units, places, acc):
    n = len(units)
    rows, _ = hamiltonian.shape
    width, nvec = units[0].shape
    first = acc is None
    nbuf = min(3, n)

    def body(places_ref, h_ref, *rest):
        unit_refs = rest[:n]
        rest = rest[n:]
        acc_ref = None
        if not first:
            acc_ref, rest = rest[0], rest[1:]
        out_ref, hbuf, ubuf, hsem, usem = rest

        def hcopy(i, slot):
            at = pl.multiple_of(places_ref[i] * width, 128)
            return pltpu.make_async_copy(h_ref.at[:, pl.ds(at, width)], hbuf.at[slot], hsem.at[slot])

        for i in range(n):
            pltpu.make_async_copy(unit_refs[i], ubuf.at[i], usem.at[i]).start()
            if i < nbuf:
                hcopy(i, i).start()
        if first:
            out_ref[...] = jnp.zeros_like(out_ref)
        else:
            out_ref[...] = acc_ref[...]

        def step(i, _):
            slot = lax.rem(i, nbuf)
            hcopy(i, slot).wait()
            pltpu.make_async_copy(unit_refs[0], ubuf.at[i], usem.at[i]).wait()
            high, low = split(hbuf[slot])
            u = ubuf[i]
            out_ref[...] += dot1(high, u) + dot1(low, u)

            @pl.when(i + nbuf < n)
            def _():
                hcopy(i + nbuf, slot).start()

            return 0

        lax.fori_loop(0, n, step, 0)

    any_spec = pl.BlockSpec(memory_space=pl.ANY)
    vmem = pl.BlockSpec(memory_space=pltpu.VMEM)
    operands = [places, hamiltonian, *units]
    in_specs = [pl.BlockSpec(memory_space=pltpu.SMEM), any_spec] + [any_spec] * n
    aliases = {}
    if not first:
        aliases = {len(operands): 0}
        operands.append(acc)
        in_specs.append(vmem)
    return pl.pallas_call(
        body,
        name="stage_product",
        out_shape=jax.ShapeDtypeStruct((rows, nvec), F32),
        in_specs=in_specs,
        out_specs=vmem,
        scratch_shapes=[
            pltpu.VMEM((nbuf, rows, width), F32),
            pltpu.VMEM((n, width, nvec), BF16),
            pltpu.SemaphoreType.DMA((nbuf,)),
            pltpu.SemaphoreType.DMA((n,)),
        ],
        input_output_aliases=aliases,
        cost_estimate=pl.CostEstimate(
            flops=4 * n * rows * width * nvec, transcendentals=0, bytes_accessed=4 * n * rows * width
        ),
        compiler_params=pltpu.CompilerParams(vmem_limit_bytes=48 << 20),
    )(*operands)


def parts_call(product, basis, own):
    rows, nvec = product.shape
    half = nvec // 2
    total = 9 * half
    piece = total // 8

    def body(own_ref, p_ref, b_ref, keep_ref, send_ref, buf):
        p = p_ref[...]
        b = b_ref[...]
        pt_high, pt_low = split(p.T)
        bt = b.astype(F32).T.astype(BF16)
        p_high, p_low = split(p)
        cross = dot1(pt_high, p_low)
        gram = dot1(pt_high, p_high) + (cross + dot1(pt_low, p_high))
        coupling = dot1(bt, p_high) + dot1(bt, p_low)
        coupling = 0.5 * (coupling + coupling.T)
        correlation = dot1(bt, b)
        at = 0
        for a in (gram, coupling, correlation):
            for i, j in ((0, 0), (1, 0), (1, 1)):
                buf[at * half:(at + 1) * half, :] = a[i * half:(i + 1) * half, j * half:(j + 1) * half]
                at += 1
        own = own_ref[0]
        for m in range(4):
            keep_ref[m] = buf[pl.ds(pl.multiple_of((own ^ m) * piece, 8), piece), :]
            send_ref[m] = buf[pl.ds(pl.multiple_of((own ^ (m + 4)) * piece, 8), piece), :]

    vmem = pl.BlockSpec(memory_space=pltpu.VMEM)
    shape = jax.ShapeDtypeStruct((4, piece, half), F32)
    return pl.pallas_call(
        body,
        name="partial_sums",
        out_shape=(shape, shape),
        in_specs=[pl.BlockSpec(memory_space=pltpu.SMEM), vmem, vmem],
        out_specs=(vmem, vmem),
        scratch_shapes=[pltpu.VMEM((total, half), F32)],
        compiler_params=pltpu.CompilerParams(vmem_limit_bytes=48 << 20),
    )(own, product, basis)


def inverse_factor(a, out_ref, work_a, work_w):
    n = a.shape[0]
    i = lax.broadcasted_iota(jnp.int32, (n, n), 0)
    j = lax.broadcasted_iota(jnp.int32, (n, n), 1)
    eye = jnp.where(i == j, 1.0, 0.0).astype(F32)
    weight = jnp.where(i > j, 1.0, jnp.where(i == j, 0.5, 0.0)).astype(F32)
    diagonal = jnp.where(i == j, a, 0.0)
    scale_row = lax.rsqrt(jnp.sum(diagonal, axis=0, keepdims=True))
    scale_col = lax.rsqrt(jnp.sum(diagonal, axis=1, keepdims=True))
    k = a * scale_row * scale_col
    e = k - eye
    x = (e * weight).astype(BF16)
    x = (e - dot1(x, x, NT)) * weight
    xh = x.astype(BF16)
    m = eye - x + dot1(xh, xh) * jnp.where(i >= j, 1.0, 0.0)

    def residual(m):
        return dot3(dot3(m, k), m, NT) - eye

    m = m - dot3(residual(m) * weight, m)
    e = residual(m)
    norm = jnp.max(jnp.sum(jnp.abs(e), axis=1))
    m = m - dot3(e * weight, m)
    out_ref[...] = m * scale_row

    @pl.when(jnp.logical_not(norm < 3e-3))
    def _():
        work_a[...] = a
        work_w[...] = eye
        lane = lax.broadcasted_iota(jnp.int32, (1, n), 1)
        row = lax.broadcasted_iota(jnp.int32, (n, 1), 0)

        def column(s, _):
            top = work_a[pl.ds(s, 1), :]
            top_w = work_w[pl.ds(s, 1), :]
            inverse = 1.0 / jnp.sum(jnp.where(lane == s, top, 0.0), axis=1, keepdims=True)
            at = work_a[...]
            col = jnp.sum(jnp.where(lane == s, at, 0.0), axis=1, keepdims=True)
            col = jnp.where(row > s, col * inverse, 0.0)
            work_a[...] = at - col * top
            work_w[...] = work_w[...] - col * top_w
            return 0

        lax.fori_loop(0, n, column, 0)
        pivots = jnp.sum(jnp.where(i == j, work_a[...], 0.0), axis=1, keepdims=True)
        out_ref[...] = work_w[...] * lax.rsqrt(pivots)


def finish_call(product, mine, other, own, scale):
    rows, nvec = product.shape
    half = nvec // 2
    _, piece, _ = mine.shape

    def body(own_ref, p_ref, mine_ref, other_ref, ritz_ref, projected_ref, buf, whole, inv, work_a, work_w):
        own = own_ref[0]
        for m in range(4):
            buf[pl.ds(pl.multiple_of((own ^ m) * piece, 8), piece), :] = mine_ref[m]
            buf[pl.ds(pl.multiple_of((own ^ (m + 4)) * piece, 8), piece), :] = other_ref[m]
        for q in range(3):
            at = 3 * q * half
            low = buf[at + half:at + 2 * half, :]
            whole[q, :half, :half] = buf[at:at + half, :]
            whole[q, half:, :half] = low
            whole[q, :half, half:] = low.T
            whole[q, half:, half:] = buf[at + 2 * half:at + 3 * half, :]
        inverse_factor(whole[0], inv.at[0], work_a, work_w)
        inverse_factor(whole[2], inv.at[1], work_a, work_w)
        ritz_ref[...] = dot3(p_ref[...], inv[0] * scale, NT)
        low = inv[1]
        projected_ref[...] = dot3(dot3(low, whole[1]), low, NT)

    vmem = pl.BlockSpec(memory_space=pltpu.VMEM)
    square = pltpu.VMEM((nvec, nvec), F32)
    return pl.pallas_call(
        body,
        name="finish",
        out_shape=(jax.ShapeDtypeStruct((rows, nvec), F32), jax.ShapeDtypeStruct((nvec, nvec), F32)),
        in_specs=[pl.BlockSpec(memory_space=pltpu.SMEM), vmem, vmem, vmem],
        out_specs=(vmem, vmem),
        scratch_shapes=[
            pltpu.VMEM((9 * half, half), F32),
            pltpu.VMEM((3, nvec, nvec), F32),
            pltpu.VMEM((2, nvec, nvec), F32),
            square,
            square,
        ],
        compiler_params=pltpu.CompilerParams(vmem_limit_bytes=48 << 20),
    )(own, product, mine, other)


STAGES = (
    ((1, 0, 1), (2, 0, 2), (4, 0, 4)),
    ((5, 4, 1), (6, 4, 2), (8, 0, 8)),
    ((3, 2, 1), (7, 5, 2), (12, 0, 12)),
    ((9, 8, 1), (10, 8, 2)),
    ((13, 12, 1), (14, 12, 2)),
    ((11, 10, 1), (15, 13, 2)),
)


def shards_pairs(hamiltonian, vectors):
    chips = lax.axis_size("rows")
    here = lax.axis_index("rows")
    core = lax.axis_index("chip")
    basis = vectors.astype(BF16)

    def from_chip(a, m):
        return lax.ppermute(a, "rows", [(s, s ^ m) for s in range(chips)])

    def from_core(a):
        return lax.ppermute(a, "chip", [(0, 1), (1, 0)])

    def places(ms):
        at = []
        for m in ms:
            at += [2 * (here ^ m) + core, 2 * (here ^ m) + 1 - core]
        return jnp.stack(at).astype(jnp.int32)

    mine = {0: basis}
    acc = None
    for stage in ((),) + STAGES:
        ms = [0] if not stage else [m for m, _, _ in stage]
        for m, source, step in stage:
            mine[m] = from_chip(mine[source], step)
        units = []
        for m in ms:
            units += [mine[m], from_core(mine[m])]
        acc = stage_call(hamiltonian, units, places(ms), acc)
    product = acc
    own = (core * 4 + here % 4).astype(jnp.int32).reshape(1)
    keep, send = parts_call(product, basis, own)
    a = keep + from_core(send)
    b = a[0] + from_chip(a[1], 1) + from_chip(a[2], 2) + from_chip(a[3], 3)
    b = b + from_chip(b, 4) + from_chip(b, 8) + from_chip(b, 12)
    mine4 = jnp.stack([b, from_chip(b, 1), from_chip(b, 2), from_chip(b, 3)])
    other4 = from_core(mine4)
    scale = float(hamiltonian.shape[1]) ** 0.5
    return finish_call(product, mine4, other4, own, scale)


def solution(mesh):
    in_specs = (P(AXES, None), P(AXES, None))
    out_specs = (P(AXES, None), P())
    pairs = mesh.shape["rows"] == 16 and mesh.shape["chip"] == 2
    body = shards_pairs if pairs else shards_plain
    return jax.shard_map(body, mesh=mesh, in_specs=in_specs, out_specs=out_specs, check_vma=False)
```

```python
import jax
import jax.numpy as jnp
from jax import lax
from jax.experimental import pallas as pl
from jax.experimental.pallas import tpu as pltpu
from jax.sharding import PartitionSpec as P


AXES = ("rows", "chip")
F32 = jnp.float32
BF16 = jnp.bfloat16
NN = (((1,), (0,)), ((), ()))
NT = (((1,), (1,)), ((), ()))


def shards_plain(hamiltonian, vectors):
    highest = lax.Precision.HIGHEST
    basis = vectors.astype(BF16)
    widened = basis.astype(F32)
    correlation_part = jnp.dot(basis.T, basis, preferred_element_type=F32)
    whole = lax.all_gather(basis, AXES, axis=0, tiled=True)
    product = jnp.dot(hamiltonian, whole.astype(F32), precision=highest)
    coupling_part = jnp.dot(widened.T, product, precision=highest)
    gram_part = jnp.dot(product.T, product, precision=highest)
    correlation, coupling, gram = lax.psum((correlation_part, coupling_part, gram_part), AXES)
    symmetric = 0.5 * (coupling + coupling.T)
    lower = jnp.linalg.cholesky(correlation)
    half = lax.linalg.triangular_solve(lower, symmetric, left_side=True, lower=True)
    projected = lax.linalg.triangular_solve(lower, half.T, left_side=True, lower=True)
    factor = jnp.linalg.cholesky(gram)
    rotated = lax.linalg.triangular_solve(factor, product.T, left_side=True, lower=True)
    return (rotated.T * jnp.sqrt(F32(hamiltonian.shape[1])), projected)


def split(a):
    high = a.astype(BF16)
    return high, (a - high.astype(F32)).astype(BF16)


def dot1(a, b, dims=NN):
    return lax.dot_general(a, b, dims, preferred_element_type=F32)


def dot3(a, b, dims=NN):
    ah, al = split(a)
    bh, bl = split(b)
    return dot1(ah, bh, dims) + (dot1(ah, bl, dims) + dot1(al, bh, dims))


def stage_call(hamiltonian, units, places, acc):
    n = len(units)
    rows, _ = hamiltonian.shape
    width = sum(a.shape[0] for a in units[0])
    nvec = units[0][0].shape[1]
    first = acc is None
    nbuf = min(3, n)
    pieces = []
    for i, unit in enumerate(units):
        at = 0
        for a in unit:
            pieces.append((i, at, a))
            at += a.shape[0]
    count = len(pieces)

    def body(places_ref, h_ref, *rest):
        piece_refs = rest[:count]
        rest = rest[count:]
        acc_refs = ()
        if not first:
            acc_refs, rest = rest[:2], rest[2:]
        out_ref, corr_ref, hbuf, ubuf, hsem, usem = rest

        def hcopy(i, slot):
            at = pl.multiple_of(places_ref[i] * width, 128)
            return pltpu.make_async_copy(h_ref.at[:, pl.ds(at, width)], hbuf.at[slot], hsem.at[slot])

        for i in range(nbuf):
            hcopy(i, i).start()
        for (i, at, a), ref in zip(pieces, piece_refs):
            pltpu.make_async_copy(ref, ubuf.at[i, pl.ds(at, a.shape[0]), :], usem.at[i]).start()
        if first:
            out_ref[...] = jnp.zeros_like(out_ref)
            corr_ref[...] = jnp.zeros_like(corr_ref)
        else:
            out_ref[...] = acc_refs[0][...]
            corr_ref[...] = acc_refs[1][...]

        def step(i, _):
            slot = lax.rem(i, nbuf)
            pltpu.make_async_copy(ubuf.at[i], ubuf.at[i], usem.at[i]).wait()
            u = ubuf[i]
            corr_ref[...] += lax.dot_general(u, u, (((0,), (0,)), ((), ())), preferred_element_type=F32)
            hcopy(i, slot).wait()
            high, low = split(hbuf[slot])
            out_ref[...] += dot1(high, u) + dot1(low, u)

            @pl.when(i + nbuf < n)
            def _():
                hcopy(i + nbuf, slot).start()

            return 0

        lax.fori_loop(0, n, step, 0)

    any_spec = pl.BlockSpec(memory_space=pl.ANY)
    vmem = pl.BlockSpec(memory_space=pltpu.VMEM)
    operands = [places, hamiltonian, *(a for _, _, a in pieces)]
    in_specs = [pl.BlockSpec(memory_space=pltpu.SMEM), any_spec] + [any_spec] * count
    aliases = {}
    if not first:
        aliases = {len(operands): 0, len(operands) + 1: 1}
        operands += list(acc)
        in_specs += [vmem, vmem]
    return pl.pallas_call(
        body,
        name="stage_product",
        out_shape=(jax.ShapeDtypeStruct((rows, nvec), F32), jax.ShapeDtypeStruct((nvec, nvec), F32)),
        in_specs=in_specs,
        out_specs=(vmem, vmem),
        scratch_shapes=[
            pltpu.VMEM((nbuf, rows, width), F32),
            pltpu.VMEM((n, width, nvec), BF16),
            pltpu.SemaphoreType.DMA((nbuf,)),
            pltpu.SemaphoreType.DMA((n,)),
        ],
        input_output_aliases=aliases,
        cost_estimate=pl.CostEstimate(
            flops=4 * n * rows * width * nvec, transcendentals=0, bytes_accessed=4 * n * rows * width
        ),
        compiler_params=pltpu.CompilerParams(vmem_limit_bytes=48 << 20),
    )(*operands)


def parts_call(product, basis, own):
    _, nvec = product.shape
    half = nvec // 2
    total = 6 * half
    piece = total // 8

    def body(own_ref, p_ref, b_ref, keep_ref, send_ref, buf):
        p = p_ref[...]
        pt_high, pt_low = split(p.T)
        bt = b_ref[...].astype(F32).T.astype(BF16)
        p_high, p_low = split(p)
        cross = dot1(pt_high, p_low)
        gram = dot1(pt_high, p_high) + (cross + dot1(pt_low, p_high))
        coupling = dot1(bt, p_high) + dot1(bt, p_low)
        coupling = 0.5 * (coupling + coupling.T)
        at = 0
        for a in (gram, coupling):
            for i, j in ((0, 0), (1, 0), (1, 1)):
                buf[at * half:(at + 1) * half, :] = a[i * half:(i + 1) * half, j * half:(j + 1) * half]
                at += 1
        own = own_ref[0]
        for m in range(4):
            keep_ref[m] = buf[pl.ds(pl.multiple_of((own ^ m) * piece, 8), piece), :]
            send_ref[m] = buf[pl.ds(pl.multiple_of((own ^ (m + 4)) * piece, 8), piece), :]

    vmem = pl.BlockSpec(memory_space=pltpu.VMEM)
    shape = jax.ShapeDtypeStruct((4, piece, half), F32)
    return pl.pallas_call(
        body,
        name="partial_sums",
        out_shape=(shape, shape),
        in_specs=[pl.BlockSpec(memory_space=pltpu.SMEM), vmem, vmem],
        out_specs=(vmem, vmem),
        scratch_shapes=[pltpu.VMEM((total, half), F32)],
        compiler_params=pltpu.CompilerParams(vmem_limit_bytes=48 << 20),
    )(own, product, basis)


def inverse_factor(a, out_ref, work_a, work_w):
    n = a.shape[0]
    i = lax.broadcasted_iota(jnp.int32, (n, n), 0)
    j = lax.broadcasted_iota(jnp.int32, (n, n), 1)
    eye = jnp.where(i == j, 1.0, 0.0).astype(F32)
    weight = jnp.where(i > j, 1.0, jnp.where(i == j, 0.5, 0.0)).astype(F32)
    diagonal = jnp.where(i == j, a, 0.0)
    scale_row = lax.rsqrt(jnp.sum(diagonal, axis=0, keepdims=True))
    scale_col = lax.rsqrt(jnp.sum(diagonal, axis=1, keepdims=True))
    k = a * scale_row * scale_col
    e = k - eye
    x = (e * weight).astype(BF16)
    x = (e - dot1(x, x, NT)) * weight
    xh = x.astype(BF16)
    m = eye - x + dot1(xh, xh) * jnp.where(i >= j, 1.0, 0.0)

    def residual(m):
        return dot3(dot3(m, k), m, NT) - eye

    m = m - dot3(residual(m) * weight, m)
    e = residual(m)
    norm = jnp.max(jnp.sum(jnp.abs(e), axis=1))
    m = m - dot3(e * weight, m)
    out_ref[...] = m * scale_row

    @pl.when(jnp.logical_not(norm < 3e-3))
    def _():
        work_a[...] = a
        work_w[...] = eye
        lane = lax.broadcasted_iota(jnp.int32, (1, n), 1)
        row = lax.broadcasted_iota(jnp.int32, (n, 1), 0)

        def column(s, _):
            top = work_a[pl.ds(s, 1), :]
            top_w = work_w[pl.ds(s, 1), :]
            inverse = 1.0 / jnp.sum(jnp.where(lane == s, top, 0.0), axis=1, keepdims=True)
            at = work_a[...]
            col = jnp.sum(jnp.where(lane == s, at, 0.0), axis=1, keepdims=True)
            col = jnp.where(row > s, col * inverse, 0.0)
            work_a[...] = at - col * top
            work_w[...] = work_w[...] - col * top_w
            return 0

        lax.fori_loop(0, n, column, 0)
        pivots = jnp.sum(jnp.where(i == j, work_a[...], 0.0), axis=1, keepdims=True)
        out_ref[...] = work_w[...] * lax.rsqrt(pivots)


def inverse_call(a):
    vmem = pl.BlockSpec(memory_space=pltpu.VMEM)
    square = pltpu.VMEM(a.shape, F32)

    def body(a_ref, out_ref, work_a, work_w):
        inverse_factor(a_ref[...], out_ref, work_a, work_w)

    return pl.pallas_call(
        body,
        name="inverse_factor",
        out_shape=jax.ShapeDtypeStruct(a.shape, F32),
        in_specs=[vmem],
        out_specs=vmem,
        scratch_shapes=[square, square],
        cost_estimate=pl.CostEstimate(flops=60 * a.shape[0] ** 3, transcendentals=0, bytes_accessed=0),
    )(a)


def finish_call(product, mine, other, low, own, scale):
    rows, nvec = product.shape
    half = nvec // 2
    _, piece, _ = mine.shape

    def body(own_ref, p_ref, mine_ref, other_ref, low_ref, ritz_ref, projected_ref, buf, whole, inv, work_a, work_w):
        own = own_ref[0]
        for m in range(4):
            buf[pl.ds(pl.multiple_of((own ^ m) * piece, 8), piece), :] = mine_ref[m]
            buf[pl.ds(pl.multiple_of((own ^ (m + 4)) * piece, 8), piece), :] = other_ref[m]
        for q in range(2):
            at = 3 * q * half
            corner = buf[at + half:at + 2 * half, :]
            whole[q, :half, :half] = buf[at:at + half, :]
            whole[q, half:, :half] = corner
            whole[q, :half, half:] = corner.T
            whole[q, half:, half:] = buf[at + 2 * half:at + 3 * half, :]
        inverse_factor(whole[0], inv, work_a, work_w)
        ritz_ref[...] = dot3(p_ref[...], inv[...] * scale, NT)
        low = low_ref[...]
        projected_ref[...] = dot3(dot3(low, whole[1]), low, NT)

    vmem = pl.BlockSpec(memory_space=pltpu.VMEM)
    square = pltpu.VMEM((nvec, nvec), F32)
    return pl.pallas_call(
        body,
        name="finish",
        out_shape=(jax.ShapeDtypeStruct((rows, nvec), F32), jax.ShapeDtypeStruct((nvec, nvec), F32)),
        in_specs=[pl.BlockSpec(memory_space=pltpu.SMEM), vmem, vmem, vmem, vmem],
        out_specs=(vmem, vmem),
        scratch_shapes=[
            pltpu.VMEM((6 * half, half), F32),
            pltpu.VMEM((2, nvec, nvec), F32),
            square,
            square,
            square,
        ],
        compiler_params=pltpu.CompilerParams(vmem_limit_bytes=48 << 20),
    )(own, product, mine, other, low)


WHOLE = (0, 8)
STAGES = (
    ((4, ((0, 4, WHOLE),)), (1, ((0, 1, WHOLE),)), (2, ((0, 2, WHOLE),))),
    ((5, ((4, 1, WHOLE),)), (6, ((4, 2, WHOLE),)), (8, ((0, 8, WHOLE),)), (3, ((2, 1, WHOLE),))),
    ((7, ((5, 2, WHOLE),)),),
    ((12, ((8, 4, WHOLE),)), (9, ((8, 1, WHOLE),)), (10, ((8, 2, WHOLE),))),
    ((14, ((12, 2, WHOLE),)), (13, ((9, 4, WHOLE),)), (11, ((10, 1, WHOLE),))),
    ((15, ((14, 1, (0, 4)), (13, 2, (4, 8)))),),
)
TURNS = (
    ((0,), ()),
    ((4, 1, 2), (0,)),
    ((5, 6), (4, 1, 2)),
    ((8, 3, 7), (5, 6)),
    ((12, 9, 10), (8, 3, 7)),
    ((14, 13, 11), (12, 9, 10)),
    ((15,), (14, 13, 11)),
    ((), (15,)),
)


def shards_pairs(hamiltonian, vectors):
    chips = lax.axis_size("rows")
    here = lax.axis_index("rows")
    core = lax.axis_index("chip")
    width = vectors.shape[0]

    def from_chip(a, m):
        return lax.ppermute(a, "rows", [(s, s ^ m) for s in range(chips)])

    def from_core(a):
        return lax.ppermute(a, "chip", [(0, 1), (1, 0)])

    basis = vectors.astype(BF16)
    mine = {0: (basis,)}
    acc = None
    other = {}
    for t, (near, far) in enumerate(TURNS):
        if 0 < t <= len(STAGES):
            for m, parts in STAGES[t - 1]:
                got = []
                for source, step, (lo, hi) in parts:
                    a = mine[source][0]
                    if (lo, hi) != WHOLE:
                        a = a[lo * width // 8:hi * width // 8]
                    got.append(from_chip(a, step))
                mine[m] = tuple(got)
        for m in near:
            other[m] = tuple(from_core(a) for a in mine[m])
        units = [mine[m] for m in near] + [other[m] for m in far]
        ids = jnp.array([2 * m for m in near] + [2 * m + 1 for m in far], jnp.int32)
        acc = stage_call(hamiltonian, units, (2 * here + core) ^ ids, acc)
    product, correlation = acc
    own = (core * 4 + here % 4).astype(jnp.int32).reshape(1)
    keep, send = parts_call(product, basis, own)
    a = keep + from_core(send)
    b = a[0] + from_chip(a[1], 1) + from_chip(a[2], 2) + from_chip(a[3], 3)
    b = b + from_chip(b, 4) + from_chip(b, 8) + from_chip(b, 12)
    mine4 = jnp.stack([b, from_chip(b, 1), from_chip(b, 2), from_chip(b, 3)])
    other4 = from_core(mine4)
    low = inverse_call(correlation)
    scale = float(hamiltonian.shape[1]) ** 0.5
    return finish_call(product, mine4, other4, low, own, scale)


def solution(mesh):
    in_specs = (P(AXES, None), P(AXES, None))
    out_specs = (P(AXES, None), P())
    pairs = mesh.shape["rows"] == 16 and mesh.shape["chip"] == 2
    body = shards_pairs if pairs else shards_plain
    return jax.shard_map(body, mesh=mesh, in_specs=in_specs, out_specs=out_specs, check_vma=False)
```

```python
import jax
import jax.numpy as jnp
from jax import lax
from jax.experimental import pallas as pl
from jax.experimental.pallas import tpu as pltpu
from jax.sharding import PartitionSpec as P


AXES = ("rows", "chip")
F32 = jnp.float32
BF16 = jnp.bfloat16
NN = (((1,), (0,)), ((), ()))
NT = (((1,), (1,)), ((), ()))


def shards_plain(hamiltonian, vectors):
    highest = lax.Precision.HIGHEST
    basis = vectors.astype(BF16)
    widened = basis.astype(F32)
    correlation_part = jnp.dot(basis.T, basis, preferred_element_type=F32)
    whole = lax.all_gather(basis, AXES, axis=0, tiled=True)
    product = jnp.dot(hamiltonian, whole.astype(F32), precision=highest)
    coupling_part = jnp.dot(widened.T, product, precision=highest)
    gram_part = jnp.dot(product.T, product, precision=highest)
    correlation, coupling, gram = lax.psum((correlation_part, coupling_part, gram_part), AXES)
    symmetric = 0.5 * (coupling + coupling.T)
    lower = jnp.linalg.cholesky(correlation)
    half = lax.linalg.triangular_solve(lower, symmetric, left_side=True, lower=True)
    projected = lax.linalg.triangular_solve(lower, half.T, left_side=True, lower=True)
    factor = jnp.linalg.cholesky(gram)
    rotated = lax.linalg.triangular_solve(factor, product.T, left_side=True, lower=True)
    return (rotated.T * jnp.sqrt(F32(hamiltonian.shape[1])), projected)


def split(a):
    high = a.astype(BF16)
    return high, (a - high.astype(F32)).astype(BF16)


def dot1(a, b, dims=NN):
    return lax.dot_general(a, b, dims, preferred_element_type=F32)


def dot3(a, b, dims=NN):
    ah, al = split(a)
    bh, bl = split(b)
    return dot1(ah, bh, dims) + (dot1(ah, bl, dims) + dot1(al, bh, dims))


def piece_at(quarter, core, slot):
    step = (0, 2 - core, 1 + core, 3)[slot]
    return 4 * core + (quarter ^ step)


def cut_pieces(p, b, quarter, core, buf, keep_ref, send_ref):
    half = p.shape[1] // 2
    piece = buf.shape[0] // 8
    pt_high, pt_low = split(p.T)
    bt = b.astype(F32).T.astype(BF16)
    p_high, p_low = split(p)
    cross = dot1(pt_high, p_low)
    gram = dot1(pt_high, p_high) + (cross + dot1(pt_low, p_high))
    coupling = dot1(bt, p_high) + dot1(bt, p_low)
    coupling = 0.5 * (coupling + coupling.T)
    correlation = dot1(bt, b)
    at = 0
    for a in (gram, coupling, correlation):
        for i, j in ((0, 0), (1, 0), (1, 1)):
            buf[at * half:(at + 1) * half, :] = a[i * half:(i + 1) * half, j * half:(j + 1) * half]
            at += 1
    for slot in range(4):
        at = pl.multiple_of(piece_at(quarter, core, slot) * piece, 8)
        keep_ref[slot] = buf[pl.ds(at, piece), :]
        at = pl.multiple_of(piece_at(quarter, 1 - core, slot) * piece, 8)
        send_ref[slot] = buf[pl.ds(at, piece), :]


def stage_call(hamiltonian, units, places, offset, acc, basis=None):
    n = len(units)
    rows, _ = hamiltonian.shape
    width = sum(a.shape[0] for a in units[0])
    nvec = units[0][0].shape[1]
    half = nvec // 2
    first = acc is None
    last = basis is not None
    nbuf = min(5, n)
    pieces = []
    for i, unit in enumerate(units):
        at = 0
        for a in unit:
            pieces.append((i, at, a))
            at += a.shape[0]
    count = len(pieces)
    tail = places.shape[0] - 2

    def body(places_ref, h_ref, *rest):
        piece_refs, rest = rest[:count], rest[count:]
        if not first:
            acc_ref, rest = rest[0], rest[1:]
        if last:
            b_ref, out_ref, keep_ref, send_ref, hbuf, ubuf, hsem, usem, buf = rest
        else:
            out_ref, hbuf, ubuf, hsem, usem = rest

        def hcopy(i, slot):
            at = pl.multiple_of(places_ref[offset + i] * width, 128)
            return pltpu.make_async_copy(h_ref.at[:, pl.ds(at, width)], hbuf.at[slot], hsem.at[slot])

        for i in range(nbuf):
            hcopy(i, i).start()
            for (k, at, a), ref in zip(pieces, piece_refs):
                if k == i or (k > i and i == nbuf - 1):
                    pltpu.make_async_copy(ref, ubuf.at[k, pl.ds(at, a.shape[0]), :], usem.at[k]).start()
        if first:
            out_ref[...] = jnp.zeros_like(out_ref)
        else:
            out_ref[...] = acc_ref[...]

        def step(i, _):
            slot = lax.rem(i, nbuf)
            pltpu.make_async_copy(ubuf.at[i], ubuf.at[i], usem.at[i]).wait()
            hcopy(i, slot).wait()
            high, low = split(hbuf[slot])
            u = ubuf[i]
            out_ref[...] += dot1(high, u) + dot1(low, u)

            @pl.when(i + nbuf < n)
            def _():
                hcopy(i + nbuf, slot).start()

            return 0

        lax.fori_loop(0, n, step, 0)
        if last:
            cut_pieces(out_ref[...], b_ref[...], places_ref[tail], places_ref[tail + 1], buf, keep_ref, send_ref)

    any_spec = pl.BlockSpec(memory_space=pl.ANY)
    vmem = pl.BlockSpec(memory_space=pltpu.VMEM)
    operands = [places, hamiltonian, *(a for _, _, a in pieces)]
    in_specs = [pl.BlockSpec(memory_space=pltpu.SMEM), any_spec] + [any_spec] * count
    aliases = {}
    if not first:
        aliases = {len(operands): 0}
        operands.append(acc)
        in_specs.append(vmem)
    out_shape = [jax.ShapeDtypeStruct((rows, nvec), F32)]
    scratch = [
        pltpu.VMEM((nbuf, rows, width), F32),
        pltpu.VMEM((n, width, nvec), BF16),
        pltpu.SemaphoreType.DMA((nbuf,)),
        pltpu.SemaphoreType.DMA((n,)),
    ]
    if last:
        operands.append(basis)
        in_specs.append(vmem)
        out_shape += [jax.ShapeDtypeStruct((4, 9 * half // 8, half), F32)] * 2
        scratch.append(pltpu.VMEM((9 * half, half), F32))
    return pl.pallas_call(
        body,
        name="stage_product",
        out_shape=tuple(out_shape),
        in_specs=in_specs,
        out_specs=(vmem,) * len(out_shape),
        scratch_shapes=scratch,
        input_output_aliases=aliases,
        cost_estimate=pl.CostEstimate(
            flops=4 * n * rows * width * nvec, transcendentals=0, bytes_accessed=4 * n * rows * width
        ),
        compiler_params=pltpu.CompilerParams(vmem_limit_bytes=48 << 20),
    )(*operands)


def refine(a):
    n = a.shape[0]
    i = lax.broadcasted_iota(jnp.int32, (n, n), 0)
    j = lax.broadcasted_iota(jnp.int32, (n, n), 1)
    eye = jnp.where(i == j, 1.0, 0.0).astype(F32)
    weight = jnp.where(i > j, 1.0, jnp.where(i == j, 0.5, 0.0)).astype(F32)
    diagonal = jnp.where(i == j, a, 0.0)
    scale_row = lax.rsqrt(jnp.sum(diagonal, axis=0, keepdims=True))
    scale_col = lax.rsqrt(jnp.sum(diagonal, axis=1, keepdims=True))
    k = a * scale_row * scale_col
    e = k - eye
    x = (e * weight).astype(BF16)
    x = (e - dot1(x, x, NT)) * weight
    xh = x.astype(BF16)
    m = eye - x + dot1(xh, xh) * jnp.where(i >= j, 1.0, 0.0)

    def residual(m):
        return dot3(dot3(m, k), m, NT) - eye

    m = m - dot3(residual(m) * weight, m)
    e = residual(m)
    norm = jnp.max(jnp.sum(jnp.abs(e), axis=1))
    m = m - dot3(e * weight, m)
    return m * scale_row, norm


def eliminate(a, out_ref, work_a, work_w):
    n = a.shape[0]
    i = lax.broadcasted_iota(jnp.int32, (n, n), 0)
    j = lax.broadcasted_iota(jnp.int32, (n, n), 1)
    work_a[...] = a
    work_w[...] = jnp.where(i == j, 1.0, 0.0).astype(F32)
    lane = lax.broadcasted_iota(jnp.int32, (1, n), 1)
    row = lax.broadcasted_iota(jnp.int32, (n, 1), 0)

    def column(s, _):
        top = work_a[pl.ds(s, 1), :]
        top_w = work_w[pl.ds(s, 1), :]
        inverse = 1.0 / jnp.sum(jnp.where(lane == s, top, 0.0), axis=1, keepdims=True)
        at = work_a[...]
        col = jnp.sum(jnp.where(lane == s, at, 0.0), axis=1, keepdims=True)
        col = jnp.where(row > s, col * inverse, 0.0)
        work_a[...] = at - col * top
        work_w[...] = work_w[...] - col * top_w
        return 0

    lax.fori_loop(0, n, column, 0)
    pivots = jnp.sum(jnp.where(i == j, work_a[...], 0.0), axis=1, keepdims=True)
    out_ref[...] = work_w[...] * lax.rsqrt(pivots)


def finish_call(product, mine, other, places, scale):
    rows, nvec = product.shape
    half = nvec // 2
    _, piece, _ = mine.shape
    tail = places.shape[0] - 2

    def body(places_ref, p_ref, mine_ref, other_ref, ritz_ref, projected_ref, pbuf, buf, whole, inv, work_a, work_w, sem):
        copy = pltpu.make_async_copy(p_ref, pbuf, sem)
        copy.start()
        quarter = places_ref[tail]
        core = places_ref[tail + 1]
        for slot in range(4):
            buf[pl.ds(pl.multiple_of(piece_at(quarter, core, slot) * piece, 8), piece), :] = mine_ref[slot]
            buf[pl.ds(pl.multiple_of(piece_at(quarter, 1 - core, slot) * piece, 8), piece), :] = other_ref[slot]
        for q in range(3):
            at = 3 * q * half
            corner = buf[at + half:at + 2 * half, :]
            whole[q, :half, :half] = buf[at:at + half, :]
            whole[q, half:, :half] = corner
            whole[q, :half, half:] = corner.T
            whole[q, half:, half:] = buf[at + 2 * half:at + 3 * half, :]
        inv[0], gram_norm = refine(whole[0])
        inv[1], correlation_norm = refine(whole[2])
        for at, source, norm in ((0, 0, gram_norm), (1, 2, correlation_norm)):
            @pl.when(jnp.logical_not(norm < 3e-3))
            def _():
                eliminate(whole[source], inv.at[at], work_a, work_w)
        copy.wait()
        ritz_ref[...] = dot3(pbuf[...], inv[0] * scale, NT)
        low = inv[1]
        projected_ref[...] = dot3(dot3(low, whole[1]), low, NT)

    vmem = pl.BlockSpec(memory_space=pltpu.VMEM)
    square = pltpu.VMEM((nvec, nvec), F32)
    return pl.pallas_call(
        body,
        name="finish",
        out_shape=(jax.ShapeDtypeStruct((rows, nvec), F32), jax.ShapeDtypeStruct((nvec, nvec), F32)),
        in_specs=[pl.BlockSpec(memory_space=pltpu.SMEM), pl.BlockSpec(memory_space=pl.ANY), vmem, vmem],
        out_specs=(vmem, vmem),
        scratch_shapes=[
            pltpu.VMEM((rows, nvec), F32),
            pltpu.VMEM((9 * half, half), F32),
            pltpu.VMEM((3, nvec, nvec), F32),
            pltpu.VMEM((2, nvec, nvec), F32),
            square,
            square,
            pltpu.SemaphoreType.DMA,
        ],
        compiler_params=pltpu.CompilerParams(vmem_limit_bytes=48 << 20),
    )(places, product, mine, other)


WHOLE = (0, 8)
STAGES = (
    ((4, ((0, 4, WHOLE),)), (1, ((0, 1, WHOLE),)), (2, ((0, 2, WHOLE),))),
    ((5, ((4, 1, WHOLE),)), (6, ((4, 2, WHOLE),)), (8, ((0, 8, WHOLE),)), (3, ((2, 1, WHOLE),))),
    ((7, ((5, 2, WHOLE),)),),
    ((12, ((8, 4, WHOLE),)), (9, ((8, 1, WHOLE),)), (10, ((8, 2, WHOLE),))),
    ((14, ((12, 2, WHOLE),)), (13, ((9, 4, WHOLE),)), (11, ((10, 1, WHOLE),))),
    ((15, ((14, 1, (0, 4)), (13, 2, (4, 8)))),),
)
TURNS = (
    ((0,), ()),
    ((4, 1, 2), (0,)),
    ((5, 6), (4, 1, 2)),
    ((8, 3, 7), (5, 6)),
    ((12, 9, 10), (8, 3, 7)),
    ((14, 13, 11), (12, 9, 10)),
    ((15,), (14, 13, 11)),
    ((), (15,)),
)


def shards_pairs(hamiltonian, vectors):
    chips = lax.axis_size("rows")
    here = lax.axis_index("rows")
    core = lax.axis_index("chip")
    width = vectors.shape[0]

    def from_chip(a, m):
        return lax.ppermute(a, "rows", [(s, s ^ m) for s in range(chips)])

    def from_core(a):
        return lax.ppermute(a, "chip", [(0, 1), (1, 0)])

    def spread(a, steps):
        return lax.ppermute(a, AXES, [(2 * s + c, 2 * (s ^ steps[c]) + c) for s in range(chips) for c in range(2)])

    basis = vectors.astype(BF16)
    order = [2 * m + far for turn in TURNS for far in range(2) for m in turn[far]]
    places = jnp.concatenate(
        [(2 * here + core) ^ jnp.array(order, jnp.int32), jnp.stack([here % 4, core]).astype(jnp.int32)]
    )
    mine = {0: (basis,)}
    acc = None
    other = {}
    offset = 0
    for t, (near, far) in enumerate(TURNS):
        if 0 < t <= len(STAGES):
            for m, parts in STAGES[t - 1]:
                got = []
                for source, step, (lo, hi) in parts:
                    a = mine[source][0]
                    if (lo, hi) != WHOLE:
                        a = a[lo * width // 8:hi * width // 8]
                    got.append(from_chip(a, step))
                mine[m] = tuple(got)
        for m in near:
            other[m] = tuple(from_core(a) for a in mine[m])
        units = [mine[m] for m in near] + [other[m] for m in far]
        end = basis if t == len(TURNS) - 1 else None
        acc, *pieces = stage_call(hamiltonian, units, places, offset, acc, end)
        offset += len(units)
    keep, send = pieces
    a = keep + from_core(send)
    a = a[:2] + spread(a[2:], (1, 2))
    a = a[:1] + spread(a[1:], (2, 1))
    a = a + spread(a, (4, 8))
    a = a + spread(a, (8, 4))
    a = jnp.concatenate([a, spread(a, (2, 1))])
    a = jnp.concatenate([a, spread(a, (1, 2))])
    b = from_core(a)
    return finish_call(acc, a, b, places, float(hamiltonian.shape[1]) ** 0.5)


def solution(mesh):
    in_specs = (P(AXES, None), P(AXES, None))
    out_specs = (P(AXES, None), P())
    pairs = mesh.shape["rows"] == 16 and mesh.shape["chip"] == 2
    body = shards_pairs if pairs else shards_plain
    return jax.shard_map(body, mesh=mesh, in_specs=in_specs, out_specs=out_specs, check_vma=False)
```

```python
import jax
import jax.numpy as jnp
from jax import lax
from jax.experimental import pallas as pl
from jax.experimental.pallas import tpu as pltpu
from jax.sharding import PartitionSpec as P


AXES = ("rows", "chip")
F32 = jnp.float32
BF16 = jnp.bfloat16
NN = (((1,), (0,)), ((), ()))
NT = (((1,), (1,)), ((), ()))


def shards_plain(hamiltonian, vectors):
    highest = lax.Precision.HIGHEST
    basis = vectors.astype(BF16)
    widened = basis.astype(F32)
    correlation_part = jnp.dot(basis.T, basis, preferred_element_type=F32)
    whole = lax.all_gather(basis, AXES, axis=0, tiled=True)
    product = jnp.dot(hamiltonian, whole.astype(F32), precision=highest)
    coupling_part = jnp.dot(widened.T, product, precision=highest)
    gram_part = jnp.dot(product.T, product, precision=highest)
    correlation, coupling, gram = lax.psum((correlation_part, coupling_part, gram_part), AXES)
    symmetric = 0.5 * (coupling + coupling.T)
    lower = jnp.linalg.cholesky(correlation)
    half = lax.linalg.triangular_solve(lower, symmetric, left_side=True, lower=True)
    projected = lax.linalg.triangular_solve(lower, half.T, left_side=True, lower=True)
    factor = jnp.linalg.cholesky(gram)
    rotated = lax.linalg.triangular_solve(factor, product.T, left_side=True, lower=True)
    return (rotated.T * jnp.sqrt(F32(hamiltonian.shape[1])), projected)


def split(a):
    high = a.astype(BF16)
    return high, (a - high.astype(F32)).astype(BF16)


def dot1(a, b, dims=NN):
    return lax.dot_general(a, b, dims, preferred_element_type=F32)


def dot3(a, b, dims=NN):
    ah, al = split(a)
    bh, bl = split(b)
    return dot1(ah, bh, dims) + (dot1(ah, bl, dims) + dot1(al, bh, dims))


def cut_pieces(p, b, own, buf, keep_ref, send_ref):
    half = p.shape[1] // 2
    piece = buf.shape[0] // 8
    pt_high, pt_low = split(p.T)
    bt = b.astype(F32).T.astype(BF16)
    p_high, p_low = split(p)
    cross = dot1(pt_high, p_low)
    gram = dot1(pt_high, p_high) + (cross + dot1(pt_low, p_high))
    coupling = dot1(bt, p_high) + dot1(bt, p_low)
    coupling = 0.5 * (coupling + coupling.T)
    at = 0
    for a in (gram, coupling):
        for i, j in ((0, 0), (1, 0), (1, 1)):
            buf[at * half:(at + 1) * half, :] = a[i * half:(i + 1) * half, j * half:(j + 1) * half]
            at += 1
    for m in range(4):
        keep_ref[m] = buf[pl.ds(pl.multiple_of((own ^ m) * piece, 8), piece), :]
        send_ref[m] = buf[pl.ds(pl.multiple_of((own ^ (m + 4)) * piece, 8), piece), :]


def stage_call(hamiltonian, units, near, places, offset, acc, basis=None):
    n = len(units)
    rows, _ = hamiltonian.shape
    width = sum(a.shape[0] for a in units[0])
    nvec = units[0][0].shape[1]
    half = nvec // 2
    first = acc is None
    last = basis is not None
    nbuf = min(5, n)
    pieces = []
    for i, unit in enumerate(units):
        at = 0
        for a in unit:
            pieces.append((i, at, a))
            at += a.shape[0]
    count = len(pieces)
    tail = places.shape[0] - 1

    def body(places_ref, h_ref, *rest):
        piece_refs, rest = rest[:count], rest[count:]
        if last:
            acc_ref, b_ref, out_ref, keep_ref, send_ref, hbuf, ubuf, hsem, usem, buf = rest
        elif first:
            out_ref, corr_ref, hbuf, ubuf, hsem, usem = rest
        else:
            acc_ref, acc_corr_ref, out_ref, corr_ref, hbuf, ubuf, hsem, usem = rest

        def hcopy(i, slot):
            at = pl.multiple_of(places_ref[offset + i] * width, 128)
            return pltpu.make_async_copy(h_ref.at[:, pl.ds(at, width)], hbuf.at[slot], hsem.at[slot])

        for i in range(nbuf):
            hcopy(i, i).start()
            for (k, at, a), ref in zip(pieces, piece_refs):
                if k == i or (k > i and i == nbuf - 1):
                    pltpu.make_async_copy(ref, ubuf.at[k, pl.ds(at, a.shape[0]), :], usem.at[k]).start()
        if first:
            out_ref[...] = jnp.zeros_like(out_ref)
            corr_ref[...] = jnp.zeros_like(corr_ref)
        else:
            out_ref[...] = acc_ref[...]
            if not last:
                corr_ref[...] = acc_corr_ref[...]

        def step(i, _):
            slot = lax.rem(i, nbuf)
            pltpu.make_async_copy(ubuf.at[i], ubuf.at[i], usem.at[i]).wait()
            if near:
                @pl.when(i < near)
                def _():
                    u = ubuf[i]
                    corr_ref[...] += lax.dot_general(u, u, (((0,), (0,)), ((), ())), preferred_element_type=F32)

            hcopy(i, slot).wait()
            high, low = split(hbuf[slot])
            u = ubuf[i]
            out_ref[...] += dot1(high, u) + dot1(low, u)

            @pl.when(i + nbuf < n)
            def _():
                hcopy(i + nbuf, slot).start()

            return 0

        lax.fori_loop(0, n, step, 0)
        if last:
            cut_pieces(out_ref[...], b_ref[...], places_ref[tail], buf, keep_ref, send_ref)

    any_spec = pl.BlockSpec(memory_space=pl.ANY)
    vmem = pl.BlockSpec(memory_space=pltpu.VMEM)
    operands = [places, hamiltonian, *(a for _, _, a in pieces)]
    in_specs = [pl.BlockSpec(memory_space=pltpu.SMEM), any_spec] + [any_spec] * count
    aliases = {}
    if not first:
        aliases = {len(operands): 0}
        operands.append(acc[0])
        in_specs.append(vmem)
        if not last:
            aliases[len(operands)] = 1
            operands.append(acc[1])
            in_specs.append(vmem)
    out_shape = [jax.ShapeDtypeStruct((rows, nvec), F32)]
    if not last:
        out_shape.append(jax.ShapeDtypeStruct((nvec, nvec), F32))
    scratch = [
        pltpu.VMEM((nbuf, rows, width), F32),
        pltpu.VMEM((n, width, nvec), BF16),
        pltpu.SemaphoreType.DMA((nbuf,)),
        pltpu.SemaphoreType.DMA((n,)),
    ]
    if last:
        operands.append(basis)
        in_specs.append(vmem)
        out_shape += [jax.ShapeDtypeStruct((4, 6 * half // 8, half), F32)] * 2
        scratch.append(pltpu.VMEM((6 * half, half), F32))
    return pl.pallas_call(
        body,
        name="stage_product",
        out_shape=tuple(out_shape),
        in_specs=in_specs,
        out_specs=(vmem,) * len(out_shape),
        scratch_shapes=scratch,
        input_output_aliases=aliases,
        cost_estimate=pl.CostEstimate(
            flops=4 * n * rows * width * nvec, transcendentals=0, bytes_accessed=4 * n * rows * width
        ),
        compiler_params=pltpu.CompilerParams(vmem_limit_bytes=24 << 20),
    )(*operands)


def refine(a):
    n = a.shape[0]
    i = lax.broadcasted_iota(jnp.int32, (n, n), 0)
    j = lax.broadcasted_iota(jnp.int32, (n, n), 1)
    eye = jnp.where(i == j, 1.0, 0.0).astype(F32)
    weight = jnp.where(i > j, 1.0, jnp.where(i == j, 0.5, 0.0)).astype(F32)
    diagonal = jnp.where(i == j, a, 0.0)
    scale_row = lax.rsqrt(jnp.sum(diagonal, axis=0, keepdims=True))
    scale_col = lax.rsqrt(jnp.sum(diagonal, axis=1, keepdims=True))
    k = a * scale_row * scale_col
    e = k - eye
    x = (e * weight).astype(BF16)
    x = (e - dot1(x, x, NT)) * weight
    xh = x.astype(BF16)
    m = eye - x + dot1(xh, xh) * jnp.where(i >= j, 1.0, 0.0)

    def residual(m):
        return dot3(dot3(m, k), m, NT) - eye

    m = m - dot1((residual(m) * weight).astype(BF16), m.astype(BF16))
    e = residual(m)
    norm = jnp.max(jnp.sum(jnp.abs(e), axis=1))
    m = m - dot1((e * weight).astype(BF16), m.astype(BF16))
    return m * scale_row, norm


def eliminate(a, out_ref, work_a, work_w):
    n = a.shape[0]
    i = lax.broadcasted_iota(jnp.int32, (n, n), 0)
    j = lax.broadcasted_iota(jnp.int32, (n, n), 1)
    work_a[...] = a
    work_w[...] = jnp.where(i == j, 1.0, 0.0).astype(F32)
    lane = lax.broadcasted_iota(jnp.int32, (1, n), 1)
    row = lax.broadcasted_iota(jnp.int32, (n, 1), 0)

    def column(s, _):
        top = work_a[pl.ds(s, 1), :]
        top_w = work_w[pl.ds(s, 1), :]
        inverse = 1.0 / jnp.sum(jnp.where(lane == s, top, 0.0), axis=1, keepdims=True)
        at = work_a[...]
        col = jnp.sum(jnp.where(lane == s, at, 0.0), axis=1, keepdims=True)
        col = jnp.where(row > s, col * inverse, 0.0)
        work_a[...] = at - col * top
        work_w[...] = work_w[...] - col * top_w
        return 0

    lax.fori_loop(0, n, column, 0)
    pivots = jnp.sum(jnp.where(i == j, work_a[...], 0.0), axis=1, keepdims=True)
    out_ref[...] = work_w[...] * lax.rsqrt(pivots)


def inverse_factor(a_ref, out_ref, work_a, work_w):
    out_ref[...], norm = refine(a_ref[...])

    @pl.when(jnp.logical_not(norm < 3e-3))
    def _():
        eliminate(a_ref[...], out_ref, work_a, work_w)


def inverse_call(near, far):
    vmem = pl.BlockSpec(memory_space=pltpu.VMEM)
    square = pltpu.VMEM(near.shape, F32)

    def body(near_ref, far_ref, out_ref, whole, work_a, work_w):
        whole[...] = near_ref[...] + far_ref[...]
        inverse_factor(whole, out_ref, work_a, work_w)

    return pl.pallas_call(
        body,
        name="inverse_factor",
        out_shape=jax.ShapeDtypeStruct(near.shape, F32),
        in_specs=[vmem, vmem],
        out_specs=vmem,
        scratch_shapes=[square, square, square],
        cost_estimate=pl.CostEstimate(flops=60 * near.shape[0] ** 3, transcendentals=0, bytes_accessed=0),
        compiler_params=pltpu.CompilerParams(vmem_limit_bytes=12 << 20),
    )(near, far)


def finish_call(product, mine, other, low, places, scale):
    rows, nvec = product.shape
    half = nvec // 2
    _, piece, _ = mine.shape
    tail = places.shape[0] - 1

    def body(places_ref, p_ref, mine_ref, other_ref, low_ref, ritz_ref, projected_ref, pbuf, buf, whole, inv, work_a, work_w, sem):
        copy = pltpu.make_async_copy(p_ref, pbuf, sem)
        copy.start()
        own = places_ref[tail]
        for m in range(4):
            buf[pl.ds(pl.multiple_of((own ^ m) * piece, 8), piece), :] = mine_ref[m]
            buf[pl.ds(pl.multiple_of((own ^ (m + 4)) * piece, 8), piece), :] = other_ref[m]
        for q in range(2):
            at = 3 * q * half
            corner = buf[at + half:at + 2 * half, :]
            whole[q, :half, :half] = buf[at:at + half, :]
            whole[q, half:, :half] = corner
            whole[q, :half, half:] = corner.T
            whole[q, half:, half:] = buf[at + 2 * half:at + 3 * half, :]
        low = low_ref[...]
        projected_ref[...] = dot3(dot3(low, whole[1]), low, NT)
        inverse_factor(whole.at[0], inv, work_a, work_w)
        copy.wait()
        ritz_ref[...] = dot3(pbuf[...], inv[...] * scale, NT)

    vmem = pl.BlockSpec(memory_space=pltpu.VMEM)
    square = pltpu.VMEM((nvec, nvec), F32)
    return pl.pallas_call(
        body,
        name="finish",
        out_shape=(jax.ShapeDtypeStruct((rows, nvec), F32), jax.ShapeDtypeStruct((nvec, nvec), F32)),
        in_specs=[pl.BlockSpec(memory_space=pltpu.SMEM), pl.BlockSpec(memory_space=pl.ANY), vmem, vmem, vmem],
        out_specs=(vmem, vmem),
        scratch_shapes=[
            pltpu.VMEM((rows, nvec), F32),
            pltpu.VMEM((6 * half, half), F32),
            pltpu.VMEM((2, nvec, nvec), F32),
            square,
            square,
            square,
            pltpu.SemaphoreType.DMA,
        ],
        compiler_params=pltpu.CompilerParams(vmem_limit_bytes=16 << 20),
    )(places, product, mine, other, low)


WHOLE = (0, 8)
STAGES = (
    ((4, ((0, 4, WHOLE),)), (1, ((0, 1, WHOLE),)), (2, ((0, 2, WHOLE),))),
    ((5, ((4, 1, WHOLE),)), (6, ((4, 2, WHOLE),)), (8, ((0, 8, WHOLE),)), (3, ((2, 1, WHOLE),))),
    ((7, ((5, 2, WHOLE),)),),
    ((12, ((8, 4, WHOLE),)), (9, ((8, 1, WHOLE),)), (10, ((8, 2, WHOLE),))),
    ((14, ((12, 2, WHOLE),)), (13, ((9, 4, WHOLE),)), (11, ((10, 1, WHOLE),))),
    ((15, ((14, 1, (0, 4)), (13, 2, (4, 8)))),),
)
TURNS = (
    ((0,), ()),
    ((4, 1, 2), (0,)),
    ((5, 6), (4, 1, 2)),
    ((8, 3, 7), (5, 6)),
    ((12, 9, 10), (8, 3, 7)),
    ((14, 13, 11), (12, 9, 10)),
    ((15,), (14, 13, 11)),
    ((), (15,)),
)


def shards_pairs(hamiltonian, vectors):
    chips = lax.axis_size("rows")
    here = lax.axis_index("rows")
    core = lax.axis_index("chip")
    width = vectors.shape[0]

    def from_chip(a, m):
        return lax.ppermute(a, "rows", [(s, s ^ m) for s in range(chips)])

    def from_core(a):
        return lax.ppermute(a, "chip", [(0, 1), (1, 0)])

    basis = vectors.astype(BF16)
    order = [2 * m + far for turn in TURNS for far in range(2) for m in turn[far]]
    places = jnp.concatenate(
        [(2 * here + core) ^ jnp.array(order, jnp.int32), (4 * core + here % 4).astype(jnp.int32).reshape(1)]
    )
    mine = {0: (basis,)}
    acc = None
    other = {}
    offset = 0
    for t, (near, far) in enumerate(TURNS):
        if 0 < t <= len(STAGES):
            for m, parts in STAGES[t - 1]:
                got = []
                for source, step, (lo, hi) in parts:
                    a = mine[source][0]
                    if (lo, hi) != WHOLE:
                        a = a[lo * width // 8:hi * width // 8]
                    got.append(from_chip(a, step))
                mine[m] = tuple(got)
        for m in near:
            other[m] = tuple(from_core(a) for a in mine[m])
        units = [mine[m] for m in near] + [other[m] for m in far]
        end = basis if t == len(TURNS) - 1 else None
        acc = stage_call(hamiltonian, units, len(near), places, offset, acc, end)
        offset += len(units)
        if t == len(TURNS) - 2:
            correlation = acc[1]
            correlation_far = from_core(correlation)
    product, keep, send = acc
    a = keep + from_core(send)
    b = a[0] + from_chip(a[1], 1) + from_chip(a[2], 2) + from_chip(a[3], 3)
    b = b + from_chip(b, 4) + from_chip(b, 8) + from_chip(b, 12)
    mine4 = jnp.stack([b, from_chip(b, 1), from_chip(b, 2), from_chip(b, 3)])
    other4 = from_core(mine4)
    low = inverse_call(correlation, correlation_far)
    return finish_call(product, mine4, other4, low, places, float(hamiltonian.shape[1]) ** 0.5)


def solution(mesh):
    in_specs = (P(AXES, None), P(AXES, None))
    out_specs = (P(AXES, None), P())
    pairs = mesh.shape["rows"] == 16 and mesh.shape["chip"] == 2
    body = shards_pairs if pairs else shards_plain
    return jax.shard_map(body, mesh=mesh, in_specs=in_specs, out_specs=out_specs, check_vma=False)
```

```python
import jax
import jax.numpy as jnp
from jax import lax
from jax.experimental import pallas as pl
from jax.experimental.pallas import tpu as pltpu
from jax.sharding import PartitionSpec as P


AXES = ("rows", "chip")
F32 = jnp.float32
BF16 = jnp.bfloat16
NN = (((1,), (0,)), ((), ()))
NT = (((1,), (1,)), ((), ()))


def shards_plain(hamiltonian, vectors):
    highest = lax.Precision.HIGHEST
    basis = vectors.astype(BF16)
    widened = basis.astype(F32)
    correlation_part = jnp.dot(basis.T, basis, preferred_element_type=F32)
    whole = lax.all_gather(basis, AXES, axis=0, tiled=True)
    product = jnp.dot(hamiltonian, whole.astype(F32), precision=highest)
    coupling_part = jnp.dot(widened.T, product, precision=highest)
    gram_part = jnp.dot(product.T, product, precision=highest)
    correlation, coupling, gram = lax.psum((correlation_part, coupling_part, gram_part), AXES)
    symmetric = 0.5 * (coupling + coupling.T)
    lower = jnp.linalg.cholesky(correlation)
    half = lax.linalg.triangular_solve(lower, symmetric, left_side=True, lower=True)
    projected = lax.linalg.triangular_solve(lower, half.T, left_side=True, lower=True)
    factor = jnp.linalg.cholesky(gram)
    rotated = lax.linalg.triangular_solve(factor, product.T, left_side=True, lower=True)
    return (rotated.T * jnp.sqrt(F32(hamiltonian.shape[1])), projected)


def split(a):
    high = a.astype(BF16)
    return high, (a - high.astype(F32)).astype(BF16)


def dot1(a, b, dims=NN):
    return lax.dot_general(a, b, dims, preferred_element_type=F32)


def dot3(a, b, dims=NN):
    ah, al = split(a)
    bh, bl = split(b)
    return dot1(ah, bh, dims) + (dot1(ah, bl, dims) + dot1(al, bh, dims))


def cut_call(product, basis, places):
    _, nvec = product.shape
    half = nvec // 2
    piece = 6 * half // 8
    tail = places.shape[0] - 1

    def body(places_ref, p_ref, b_ref, keep_ref, send_ref, buf):
        p = p_ref[...]
        own = places_ref[tail]
        pt_high, pt_low = split(p.T)
        bt = b_ref[...].astype(F32).T.astype(BF16)
        p_high, p_low = split(p)
        cross = dot1(pt_high, p_low)
        gram = dot1(pt_high, p_high) + (cross + dot1(pt_low, p_high))
        coupling = dot1(bt, p_high) + dot1(bt, p_low)
        coupling = 0.5 * (coupling + coupling.T)
        at = 0
        for a in (gram, coupling):
            for i, j in ((0, 0), (1, 0), (1, 1)):
                buf[at * half:(at + 1) * half, :] = a[i * half:(i + 1) * half, j * half:(j + 1) * half]
                at += 1
        for m in range(4):
            keep_ref[m] = buf[pl.ds(pl.multiple_of((own ^ m) * piece, 8), piece), :]
            send_ref[m] = buf[pl.ds(pl.multiple_of((own ^ (m + 4)) * piece, 8), piece), :]

    vmem = pl.BlockSpec(memory_space=pltpu.VMEM)
    shape = jax.ShapeDtypeStruct((4, piece, half), F32)
    return pl.pallas_call(
        body,
        name="cut_pieces",
        out_shape=(shape, shape),
        in_specs=[pl.BlockSpec(memory_space=pltpu.SMEM), vmem, vmem],
        out_specs=(vmem, vmem),
        scratch_shapes=[pltpu.VMEM((6 * half, half), F32)],
        compiler_params=pltpu.CompilerParams(vmem_limit_bytes=16 << 20),
    )(places, product, basis)


BUFFERS = 5


def stage_call(hamiltonian, units, near, places, offset, ready, ahead, acc):
    n = len(units)
    rows, _ = hamiltonian.shape
    width, nvec = units[0].shape
    first = acc is None
    count = 3 if near else 2

    def body(places_ref, h_ref, *rest):
        unit_refs, rest = rest[:n], rest[n:]
        if not first:
            sums, rest = rest[:count], rest[count:]
        totals, rest = rest[:count], rest[count:]
        ring, out_ref = totals[:2]
        ubuf, hsem, usem = rest

        def fetch(i):
            at = pl.multiple_of(places_ref[offset + i] * width, 128)
            slot = lax.rem(offset + i, BUFFERS)
            return pltpu.make_async_copy(h_ref.at[:, pl.ds(at, width)], ring.at[slot], hsem.at[slot])

        for i in range(n):
            if ready <= i < min(BUFFERS, n + ahead):
                fetch(i).start()
            pltpu.make_async_copy(unit_refs[i], ubuf.at[i], usem.at[i]).start()
        for i in range(n, min(BUFFERS, n + ahead)):
            fetch(i).start()
        for k in range(1, count):
            totals[k][...] = jnp.zeros_like(totals[k]) if first else sums[k][...]

        def step(i, _):
            pltpu.make_async_copy(ubuf.at[i], ubuf.at[i], usem.at[i]).wait()
            if near:
                @pl.when(i < near)
                def _():
                    u = ubuf[i]
                    totals[2][...] += lax.dot_general(u, u, (((0,), (0,)), ((), ())), preferred_element_type=F32)

            @pl.when(i >= ready)
            def _():
                fetch(i).wait()

            high, low = split(ring[lax.rem(offset + i, BUFFERS)])
            u = ubuf[i]
            out_ref[...] += dot1(high, u) + dot1(low, u)

            @pl.when(i + BUFFERS < n + ahead)
            def _():
                fetch(i + BUFFERS).start()

            return 0

        lax.fori_loop(0, n, step, 0)
        for i in range(n, n + ahead):
            fetch(i).wait()

    any_spec = pl.BlockSpec(memory_space=pl.ANY)
    vmem = pl.BlockSpec(memory_space=pltpu.VMEM)
    operands = [places, hamiltonian, *units]
    in_specs = [pl.BlockSpec(memory_space=pltpu.SMEM), any_spec] + [any_spec] * n
    aliases = {}
    if not first:
        aliases = {len(operands) + k: k for k in range(count)}
        operands += list(acc[:count])
        in_specs += [vmem] * count
    return pl.pallas_call(
        body,
        name="stage_product",
        out_shape=(
            jax.ShapeDtypeStruct((BUFFERS, rows, width), F32),
            jax.ShapeDtypeStruct((rows, nvec), F32),
            jax.ShapeDtypeStruct((nvec, nvec), F32),
        )[:count],
        in_specs=in_specs,
        out_specs=(vmem,) * count,
        scratch_shapes=[
            pltpu.VMEM((n, width, nvec), BF16),
            pltpu.SemaphoreType.DMA((BUFFERS,)),
            pltpu.SemaphoreType.DMA((n,)),
        ],
        input_output_aliases=aliases,
        cost_estimate=pl.CostEstimate(
            flops=4 * n * rows * width * nvec, transcendentals=0, bytes_accessed=4 * n * rows * width
        ),
        compiler_params=pltpu.CompilerParams(vmem_limit_bytes=8 << 20),
    )(*operands)


def refine(a):
    n = a.shape[0]
    i = lax.broadcasted_iota(jnp.int32, (n, n), 0)
    j = lax.broadcasted_iota(jnp.int32, (n, n), 1)
    eye = jnp.where(i == j, 1.0, 0.0).astype(F32)
    weight = jnp.where(i > j, 1.0, jnp.where(i == j, 0.5, 0.0)).astype(F32)
    diagonal = jnp.where(i == j, a, 0.0)
    scale_row = lax.rsqrt(jnp.sum(diagonal, axis=0, keepdims=True))
    scale_col = lax.rsqrt(jnp.sum(diagonal, axis=1, keepdims=True))
    k = a * scale_row * scale_col
    e = k - eye
    x = (e * weight).astype(BF16)
    x = (e - dot1(x, x, NT)) * weight
    xh = x.astype(BF16)
    m = eye - x + dot1(xh, xh) * jnp.where(i >= j, 1.0, 0.0)

    def residual(m):
        return dot3(dot3(m, k), m, NT) - eye

    m = m - dot1((residual(m) * weight).astype(BF16), m.astype(BF16))
    e = residual(m)
    norm = jnp.max(jnp.sum(jnp.abs(e), axis=1))
    m = m - dot1((e * weight).astype(BF16), m.astype(BF16))
    return m * scale_row, norm


def eliminate(a, out_ref, work_a, work_w):
    n = a.shape[0]
    i = lax.broadcasted_iota(jnp.int32, (n, n), 0)
    j = lax.broadcasted_iota(jnp.int32, (n, n), 1)
    work_a[...] = a
    work_w[...] = jnp.where(i == j, 1.0, 0.0).astype(F32)
    lane = lax.broadcasted_iota(jnp.int32, (1, n), 1)
    row = lax.broadcasted_iota(jnp.int32, (n, 1), 0)

    def column(s, _):
        top = work_a[pl.ds(s, 1), :]
        top_w = work_w[pl.ds(s, 1), :]
        inverse = 1.0 / jnp.sum(jnp.where(lane == s, top, 0.0), axis=1, keepdims=True)
        at = work_a[...]
        col = jnp.sum(jnp.where(lane == s, at, 0.0), axis=1, keepdims=True)
        col = jnp.where(row > s, col * inverse, 0.0)
        work_a[...] = at - col * top
        work_w[...] = work_w[...] - col * top_w
        return 0

    lax.fori_loop(0, n, column, 0)
    pivots = jnp.sum(jnp.where(i == j, work_a[...], 0.0), axis=1, keepdims=True)
    out_ref[...] = work_w[...] * lax.rsqrt(pivots)


def inverse_factor(a_ref, out_ref, work_a, work_w):
    out_ref[...], norm = refine(a_ref[...])

    @pl.when(jnp.logical_not(norm < 3e-3))
    def _():
        eliminate(a_ref[...], out_ref, work_a, work_w)


def inverse_call(near, far):
    vmem = pl.BlockSpec(memory_space=pltpu.VMEM)
    square = pltpu.VMEM(near.shape, F32)

    def body(near_ref, far_ref, out_ref, whole, work_a, work_w):
        whole[...] = near_ref[...] + far_ref[...]
        inverse_factor(whole, out_ref, work_a, work_w)

    return pl.pallas_call(
        body,
        name="inverse_factor",
        out_shape=jax.ShapeDtypeStruct(near.shape, F32),
        in_specs=[vmem, vmem],
        out_specs=vmem,
        scratch_shapes=[square, square, square],
        cost_estimate=pl.CostEstimate(flops=60 * near.shape[0] ** 3, transcendentals=0, bytes_accessed=0),
        compiler_params=pltpu.CompilerParams(vmem_limit_bytes=12 << 20),
    )(near, far)


def finish_call(product, mine, other, low, places, scale):
    rows, nvec = product.shape
    half = nvec // 2
    _, piece, _ = mine.shape
    tail = places.shape[0] - 1

    def body(places_ref, p_ref, mine_ref, other_ref, low_ref, ritz_ref, projected_ref, pbuf, buf, whole, inv, work_a, work_w, sem):
        copy = pltpu.make_async_copy(p_ref, pbuf, sem)
        copy.start()
        own = places_ref[tail]
        for m in range(4):
            buf[pl.ds(pl.multiple_of((own ^ m) * piece, 8), piece), :] = mine_ref[m]
            buf[pl.ds(pl.multiple_of((own ^ (m + 4)) * piece, 8), piece), :] = other_ref[m]
        for q in range(2):
            at = 3 * q * half
            corner = buf[at + half:at + 2 * half, :]
            whole[q, :half, :half] = buf[at:at + half, :]
            whole[q, half:, :half] = corner
            whole[q, :half, half:] = corner.T
            whole[q, half:, half:] = buf[at + 2 * half:at + 3 * half, :]
        low = low_ref[...]
        projected_ref[...] = dot3(dot3(low, whole[1]), low, NT)
        inverse_factor(whole.at[0], inv, work_a, work_w)
        copy.wait()
        ritz_ref[...] = dot3(pbuf[...], inv[...] * scale, NT)

    vmem = pl.BlockSpec(memory_space=pltpu.VMEM)
    square = pltpu.VMEM((nvec, nvec), F32)
    return pl.pallas_call(
        body,
        name="finish",
        out_shape=(jax.ShapeDtypeStruct((rows, nvec), F32), jax.ShapeDtypeStruct((nvec, nvec), F32)),
        in_specs=[pl.BlockSpec(memory_space=pltpu.SMEM), pl.BlockSpec(memory_space=pl.ANY), vmem, vmem, vmem],
        out_specs=(vmem, vmem),
        scratch_shapes=[
            pltpu.VMEM((rows, nvec), F32),
            pltpu.VMEM((6 * half, half), F32),
            pltpu.VMEM((2, nvec, nvec), F32),
            square,
            square,
            square,
            pltpu.SemaphoreType.DMA,
        ],
        compiler_params=pltpu.CompilerParams(vmem_limit_bytes=16 << 20),
    )(places, product, mine, other, low)


STAGES = (
    ((4, 0, 4), (1, 0, 1), (2, 0, 2)),
    ((5, 4, 1), (6, 4, 2), (8, 0, 8), (3, 2, 1)),
    ((7, 5, 2),),
    ((12, 8, 4), (9, 8, 1), (10, 8, 2)),
    ((14, 12, 2), (13, 9, 4), (11, 10, 1)),
    ((15, 14, 1),),
)
TURNS = (
    ((0,), (0,), 3),
    ((4, 1, 2), (), 1),
    ((5, 6), (4, 1, 2), 1),
    ((8, 3, 7), (5, 6), 1),
    ((12, 9, 10), (8, 3, 7), 1),
    ((14, 13, 11), (12, 9, 10), 1),
    ((15,), (14, 13, 11), 1),
    ((), (15,), 0),
)


def shards_pairs(hamiltonian, vectors):
    chips = lax.axis_size("rows")
    here = lax.axis_index("rows")
    core = lax.axis_index("chip")

    def from_chip(a, m):
        return lax.ppermute(a, "rows", [(s, s ^ m) for s in range(chips)])

    def from_core(a):
        return lax.ppermute(a, "chip", [(0, 1), (1, 0)])

    basis = vectors.astype(BF16)
    order = [2 * m + far for turn in TURNS for far in range(2) for m in turn[far]]
    places = jnp.concatenate(
        [(2 * here + core) ^ jnp.array(order, jnp.int32), (4 * core + here % 4).astype(jnp.int32).reshape(1)]
    )
    mine = {0: basis}
    acc = None
    other = {}
    offset = ready = 0
    for t, (near, far, ahead) in enumerate(TURNS):
        if 0 < t <= len(STAGES):
            for m, source, step in STAGES[t - 1]:
                mine[m] = from_chip(mine[source], step)
        for m in near:
            other[m] = from_core(mine[m])
        units = [mine[m] for m in near] + [other[m] for m in far]
        acc = stage_call(hamiltonian, units, len(near), places, offset, ready, ahead, acc)
        offset += len(units)
        ready = ahead
        if t == len(TURNS) - 2:
            correlation = acc[2]
            correlation_far = from_core(correlation)
    product = acc[1]
    keep, send = cut_call(product, basis, places)
    a = keep + from_core(send)
    b = a[0] + from_chip(a[1], 1) + from_chip(a[2], 2) + from_chip(a[3], 3)
    b = b + from_chip(b, 4) + from_chip(b, 8) + from_chip(b, 12)
    mine4 = jnp.stack([b, from_chip(b, 1), from_chip(b, 2), from_chip(b, 3)])
    other4 = from_core(mine4)
    low = inverse_call(correlation, correlation_far)
    return finish_call(product, mine4, other4, low, places, float(hamiltonian.shape[1]) ** 0.5)


def solution(mesh):
    in_specs = (P(AXES, None), P(AXES, None))
    out_specs = (P(AXES, None), P())
    pairs = mesh.shape["rows"] == 16 and mesh.shape["chip"] == 2
    body = shards_pairs if pairs else shards_plain
    return jax.shard_map(body, mesh=mesh, in_specs=in_specs, out_specs=out_specs, check_vma=False)
```

```python
import jax
import jax.numpy as jnp
from jax import lax
from jax.experimental import pallas as pl
from jax.experimental.pallas import tpu as pltpu
from jax.sharding import PartitionSpec as P


AXES = ("rows", "chip")
F32 = jnp.float32
BF16 = jnp.bfloat16
NN = (((1,), (0,)), ((), ()))
NT = (((1,), (1,)), ((), ()))


def shards_plain(hamiltonian, vectors):
    highest = lax.Precision.HIGHEST
    basis = vectors.astype(BF16)
    widened = basis.astype(F32)
    correlation_part = jnp.dot(basis.T, basis, preferred_element_type=F32)
    whole = lax.all_gather(basis, AXES, axis=0, tiled=True)
    product = jnp.dot(hamiltonian, whole.astype(F32), precision=highest)
    coupling_part = jnp.dot(widened.T, product, precision=highest)
    gram_part = jnp.dot(product.T, product, precision=highest)
    correlation, coupling, gram = lax.psum((correlation_part, coupling_part, gram_part), AXES)
    symmetric = 0.5 * (coupling + coupling.T)
    lower = jnp.linalg.cholesky(correlation)
    half = lax.linalg.triangular_solve(lower, symmetric, left_side=True, lower=True)
    projected = lax.linalg.triangular_solve(lower, half.T, left_side=True, lower=True)
    factor = jnp.linalg.cholesky(gram)
    rotated = lax.linalg.triangular_solve(factor, product.T, left_side=True, lower=True)
    return (rotated.T * jnp.sqrt(F32(hamiltonian.shape[1])), projected)


def split(a):
    high = a.astype(BF16)
    return high, (a - high.astype(F32)).astype(BF16)


def dot1(a, b, dims=NN):
    return lax.dot_general(a, b, dims, preferred_element_type=F32)


def dot3(a, b, dims=NN):
    ah, al = split(a)
    bh, bl = split(b)
    return dot1(ah, bh, dims) + (dot1(ah, bl, dims) + dot1(al, bh, dims))


def cut_call(product, basis, places):
    _, nvec = product.shape
    half = nvec // 2
    piece = 6 * half // 8
    tail = places.shape[0] - 1

    def body(places_ref, p_ref, b_ref, keep_ref, send_ref, buf):
        p = p_ref[...]
        own = places_ref[tail]
        pt_high, pt_low = split(p.T)
        bt = b_ref[...].astype(F32).T.astype(BF16)
        p_high, p_low = split(p)
        cross = dot1(pt_high, p_low)
        gram = dot1(pt_high, p_high) + (cross + dot1(pt_low, p_high))
        coupling = dot1(bt, p_high) + dot1(bt, p_low)
        coupling = 0.5 * (coupling + coupling.T)
        at = 0
        for a in (gram, coupling):
            for i, j in ((0, 0), (1, 0), (1, 1)):
                buf[at * half:(at + 1) * half, :] = a[i * half:(i + 1) * half, j * half:(j + 1) * half]
                at += 1
        for m in range(4):
            keep_ref[m] = buf[pl.ds(pl.multiple_of((own ^ m) * piece, 8), piece), :]
            send_ref[m] = buf[pl.ds(pl.multiple_of((own ^ (m + 4)) * piece, 8), piece), :]

    vmem = pl.BlockSpec(memory_space=pltpu.VMEM)
    shape = jax.ShapeDtypeStruct((4, piece, half), F32)
    return pl.pallas_call(
        body,
        name="cut_pieces",
        out_shape=(shape, shape),
        in_specs=[pl.BlockSpec(memory_space=pltpu.SMEM), vmem, vmem],
        out_specs=(vmem, vmem),
        scratch_shapes=[pltpu.VMEM((6 * half, half), F32)],
        compiler_params=pltpu.CompilerParams(vmem_limit_bytes=16 << 20),
    )(places, product, basis)


BUFFERS = 5


def stage_call(hamiltonian, units, near, places, offset, ready, ahead, acc):
    n = len(units)
    rows, _ = hamiltonian.shape
    width, nvec = units[0].shape
    first = acc is None
    count = 3 if near else 2

    def body(places_ref, h_ref, *rest):
        unit_refs, rest = rest[:n], rest[n:]
        if not first:
            sums, rest = rest[:count], rest[count:]
        totals, rest = rest[:count], rest[count:]
        ring, out_ref = totals[:2]
        ubuf, hsem, usem = rest

        def fetch(i):
            at = pl.multiple_of(places_ref[offset + i] * width, 128)
            slot = lax.rem(offset + i, BUFFERS)
            return pltpu.make_async_copy(h_ref.at[:, pl.ds(at, width)], ring.at[slot], hsem.at[slot])

        for i in range(n):
            if ready <= i < min(BUFFERS, n + ahead):
                fetch(i).start()
            pltpu.make_async_copy(unit_refs[i], ubuf.at[i], usem.at[i]).start()
        for i in range(n, min(BUFFERS, n + ahead)):
            fetch(i).start()
        for k in range(1, count):
            totals[k][...] = jnp.zeros_like(totals[k]) if first else sums[k][...]

        def step(i, correlate):
            pltpu.make_async_copy(ubuf.at[i], ubuf.at[i], usem.at[i]).wait()

            @pl.when(i >= ready)
            def _():
                fetch(i).wait()

            high, low = split(ring[lax.rem(offset + i, BUFFERS)])
            u = ubuf[i]
            if correlate:
                totals[2][...] += lax.dot_general(u, u, (((0,), (0,)), ((), ())), preferred_element_type=F32)
            out_ref[...] += dot1(high, u) + dot1(low, u)

            @pl.when(i + BUFFERS < n + ahead)
            def _():
                fetch(i + BUFFERS).start()

        def near_step(i, _):
            step(i, True)
            return 0

        def far_step(i, _):
            step(i, False)
            return 0

        if near:
            lax.fori_loop(0, near, near_step, 0)
        if near < n:
            lax.fori_loop(near, n, far_step, 0)
        for i in range(n, n + ahead):
            fetch(i).wait()

    any_spec = pl.BlockSpec(memory_space=pl.ANY)
    vmem = pl.BlockSpec(memory_space=pltpu.VMEM)
    operands = [places, hamiltonian, *units]
    in_specs = [pl.BlockSpec(memory_space=pltpu.SMEM), any_spec] + [any_spec] * n
    aliases = {}
    if not first:
        aliases = {len(operands) + k: k for k in range(count)}
        operands += list(acc[:count])
        in_specs += [vmem] * count
    return pl.pallas_call(
        body,
        name="stage_product",
        out_shape=(
            jax.ShapeDtypeStruct((BUFFERS, rows, width), F32),
            jax.ShapeDtypeStruct((rows, nvec), F32),
            jax.ShapeDtypeStruct((nvec, nvec), F32),
        )[:count],
        in_specs=in_specs,
        out_specs=(vmem,) * count,
        scratch_shapes=[
            pltpu.VMEM((n, width, nvec), BF16),
            pltpu.SemaphoreType.DMA((BUFFERS,)),
            pltpu.SemaphoreType.DMA((n,)),
        ],
        input_output_aliases=aliases,
        cost_estimate=pl.CostEstimate(
            flops=4 * n * rows * width * nvec, transcendentals=0, bytes_accessed=4 * n * rows * width
        ),
        compiler_params=pltpu.CompilerParams(vmem_limit_bytes=8 << 20),
    )(*operands)


def refine(a):
    n = a.shape[0]
    i = lax.broadcasted_iota(jnp.int32, (n, n), 0)
    j = lax.broadcasted_iota(jnp.int32, (n, n), 1)
    eye = jnp.where(i == j, 1.0, 0.0).astype(F32)
    weight = jnp.where(i > j, 1.0, jnp.where(i == j, 0.5, 0.0)).astype(F32)
    diagonal = jnp.where(i == j, a, 0.0)
    scale_row = lax.rsqrt(jnp.sum(diagonal, axis=0, keepdims=True))
    scale_col = lax.rsqrt(jnp.sum(diagonal, axis=1, keepdims=True))
    k = a * scale_row * scale_col
    e = k - eye
    x = (e * weight).astype(BF16)
    x = (e - dot1(x, x, NT)) * weight
    xh = x.astype(BF16)
    m = eye - x + dot1(xh, xh) * jnp.where(i >= j, 1.0, 0.0)

    def residual(m):
        return dot3(dot3(m, k), m, NT) - eye

    m = m - dot1((residual(m) * weight).astype(BF16), m.astype(BF16))
    e = residual(m)
    norm = jnp.max(jnp.sum(jnp.abs(e), axis=1))
    m = m - dot1((e * weight).astype(BF16), m.astype(BF16))
    return m * scale_row, norm


def eliminate(a, out_ref, work_a, work_w):
    n = a.shape[0]
    i = lax.broadcasted_iota(jnp.int32, (n, n), 0)
    j = lax.broadcasted_iota(jnp.int32, (n, n), 1)
    work_a[...] = a
    work_w[...] = jnp.where(i == j, 1.0, 0.0).astype(F32)
    lane = lax.broadcasted_iota(jnp.int32, (1, n), 1)
    row = lax.broadcasted_iota(jnp.int32, (n, 1), 0)

    def column(s, _):
        top = work_a[pl.ds(s, 1), :]
        top_w = work_w[pl.ds(s, 1), :]
        inverse = 1.0 / jnp.sum(jnp.where(lane == s, top, 0.0), axis=1, keepdims=True)
        at = work_a[...]
        col = jnp.sum(jnp.where(lane == s, at, 0.0), axis=1, keepdims=True)
        col = jnp.where(row > s, col * inverse, 0.0)
        work_a[...] = at - col * top
        work_w[...] = work_w[...] - col * top_w
        return 0

    lax.fori_loop(0, n, column, 0)
    pivots = jnp.sum(jnp.where(i == j, work_a[...], 0.0), axis=1, keepdims=True)
    out_ref[...] = work_w[...] * lax.rsqrt(pivots)


def inverse_factor(a_ref, out_ref, work_a, work_w):
    out_ref[...], norm = refine(a_ref[...])

    @pl.when(jnp.logical_not(norm < 3e-3))
    def _():
        eliminate(a_ref[...], out_ref, work_a, work_w)


def inverse_call(near, far):
    vmem = pl.BlockSpec(memory_space=pltpu.VMEM)
    square = pltpu.VMEM(near.shape, F32)

    def body(near_ref, far_ref, out_ref, whole, work_a, work_w):
        whole[...] = near_ref[...] + far_ref[...]
        inverse_factor(whole, out_ref, work_a, work_w)

    return pl.pallas_call(
        body,
        name="inverse_factor",
        out_shape=jax.ShapeDtypeStruct(near.shape, F32),
        in_specs=[vmem, vmem],
        out_specs=vmem,
        scratch_shapes=[square, square, square],
        cost_estimate=pl.CostEstimate(flops=60 * near.shape[0] ** 3, transcendentals=0, bytes_accessed=0),
        compiler_params=pltpu.CompilerParams(vmem_limit_bytes=12 << 20),
    )(near, far)


def finish_call(product, mine, other, low, places, scale):
    rows, nvec = product.shape
    half = nvec // 2
    _, piece, _ = mine.shape
    tail = places.shape[0] - 1

    def body(places_ref, p_ref, mine_ref, other_ref, low_ref, ritz_ref, projected_ref, pbuf, buf, whole, inv, work_a, work_w, sem):
        copy = pltpu.make_async_copy(p_ref, pbuf, sem)
        copy.start()
        own = places_ref[tail]
        for m in range(4):
            buf[pl.ds(pl.multiple_of((own ^ m) * piece, 8), piece), :] = mine_ref[m]
            buf[pl.ds(pl.multiple_of((own ^ (m + 4)) * piece, 8), piece), :] = other_ref[m]
        for q in range(2):
            at = 3 * q * half
            corner = buf[at + half:at + 2 * half, :]
            whole[q, :half, :half] = buf[at:at + half, :]
            whole[q, half:, :half] = corner
            whole[q, :half, half:] = corner.T
            whole[q, half:, half:] = buf[at + 2 * half:at + 3 * half, :]
        low = low_ref[...]
        projected_ref[...] = dot3(dot3(low, whole[1]), low, NT)
        inverse_factor(whole.at[0], inv, work_a, work_w)
        copy.wait()
        ritz_ref[...] = dot3(pbuf[...], inv[...] * scale, NT)

    vmem = pl.BlockSpec(memory_space=pltpu.VMEM)
    square = pltpu.VMEM((nvec, nvec), F32)
    return pl.pallas_call(
        body,
        name="finish",
        out_shape=(jax.ShapeDtypeStruct((rows, nvec), F32), jax.ShapeDtypeStruct((nvec, nvec), F32)),
        in_specs=[pl.BlockSpec(memory_space=pltpu.SMEM), pl.BlockSpec(memory_space=pl.ANY), vmem, vmem, vmem],
        out_specs=(vmem, vmem),
        scratch_shapes=[
            pltpu.VMEM((rows, nvec), F32),
            pltpu.VMEM((6 * half, half), F32),
            pltpu.VMEM((2, nvec, nvec), F32),
            square,
            square,
            square,
            pltpu.SemaphoreType.DMA,
        ],
        compiler_params=pltpu.CompilerParams(vmem_limit_bytes=16 << 20),
    )(places, product, mine, other, low)


STAGES = (
    ((4, 0, 4), (1, 0, 1), (2, 0, 2)),
    ((5, 4, 1), (6, 4, 2), (8, 0, 8), (3, 2, 1)),
    ((7, 5, 2),),
    ((12, 8, 4), (9, 8, 1), (10, 8, 2)),
    ((14, 12, 2), (13, 9, 4), (11, 10, 1)),
    ((15, 14, 1),),
)
TURNS = (
    ((0,), (0,), 3, (4, 1, 2)),
    ((4, 1, 2), (), 1, (5, 6, 8, 3)),
    ((), (4, 1, 2), 2, (5, 6, 8, 3)),
    ((5, 6), (), 1, (7, 8, 3)),
    ((), (5, 6), 3, (7, 8, 3)),
    ((8, 3, 7), (), 2, (12, 9, 10)),
    ((12, 9, 10), (8, 3, 7), 1, (14, 13, 11)),
    ((14, 13, 11), (12, 9, 10), 1, (15,)),
    ((), (14, 13, 11), 1, (15,)),
    ((15,), (), 1, ()),
    ((), (15,), 0, ()),
)


def shards_pairs(hamiltonian, vectors):
    chips = lax.axis_size("rows")
    here = lax.axis_index("rows")
    core = lax.axis_index("chip")

    def from_chip(a, m):
        return lax.ppermute(a, "rows", [(s, s ^ m) for s in range(chips)])

    def from_core(a):
        return lax.ppermute(a, "chip", [(0, 1), (1, 0)])

    basis = vectors.astype(BF16)
    order = [2 * m + far for turn in TURNS for far in range(2) for m in turn[far]]
    places = jnp.concatenate(
        [(2 * here + core) ^ jnp.array(order, jnp.int32), (4 * core + here % 4).astype(jnp.int32).reshape(1)]
    )
    mine = {0: basis}
    acc = None
    other = {}
    offset = ready = 0
    for stage in STAGES:
        for m, source, step in stage:
            mine[m] = from_chip(mine[source], step)
    for t, (near, far, ahead, _) in enumerate(TURNS):
        for m in near:
            other[m] = from_core(mine[m])
        units = [mine[m] for m in near] + [other[m] for m in far]
        sums = stage_call(hamiltonian, units, len(near), places, offset, ready, ahead, acc)
        acc = sums if near else (*sums, acc[2])
        offset += len(units)
        ready = ahead
        if near:
            correlation = acc[2]
        if t == len(TURNS) - 2:
            correlation_far = from_core(correlation)
    product = acc[1]
    keep, send = cut_call(product, basis, places)
    a = keep + from_core(send)
    b = a[0] + from_chip(a[1], 1) + from_chip(a[2], 2) + from_chip(a[3], 3)
    b = b + from_chip(b, 4) + from_chip(b, 8) + from_chip(b, 12)
    mine4 = jnp.stack([b, from_chip(b, 1), from_chip(b, 2), from_chip(b, 3)])
    other4 = from_core(mine4)
    low = inverse_call(correlation, correlation_far)
    return finish_call(product, mine4, other4, low, places, float(hamiltonian.shape[1]) ** 0.5)


def solution(mesh):
    in_specs = (P(AXES, None), P(AXES, None))
    out_specs = (P(AXES, None), P())
    pairs = mesh.shape["rows"] == 16 and mesh.shape["chip"] == 2
    body = shards_pairs if pairs else shards_plain
    return jax.shard_map(body, mesh=mesh, in_specs=in_specs, out_specs=out_specs, check_vma=False)
```

```python
import jax
import jax.numpy as jnp
from jax import lax
from jax.experimental import pallas as pl
from jax.experimental.pallas import tpu as pltpu
from jax.sharding import PartitionSpec as P


AXES = ("rows", "chip")
F32 = jnp.float32
BF16 = jnp.bfloat16
NN = (((1,), (0,)), ((), ()))
NT = (((1,), (1,)), ((), ()))


def shards_plain(hamiltonian, vectors):
    highest = lax.Precision.HIGHEST
    basis = vectors.astype(BF16)
    widened = basis.astype(F32)
    correlation_part = jnp.dot(basis.T, basis, preferred_element_type=F32)
    whole = lax.all_gather(basis, AXES, axis=0, tiled=True)
    product = jnp.dot(hamiltonian, whole.astype(F32), precision=highest)
    coupling_part = jnp.dot(widened.T, product, precision=highest)
    gram_part = jnp.dot(product.T, product, precision=highest)
    correlation, coupling, gram = lax.psum((correlation_part, coupling_part, gram_part), AXES)
    symmetric = 0.5 * (coupling + coupling.T)
    lower = jnp.linalg.cholesky(correlation)
    half = lax.linalg.triangular_solve(lower, symmetric, left_side=True, lower=True)
    projected = lax.linalg.triangular_solve(lower, half.T, left_side=True, lower=True)
    factor = jnp.linalg.cholesky(gram)
    rotated = lax.linalg.triangular_solve(factor, product.T, left_side=True, lower=True)
    return (rotated.T * jnp.sqrt(F32(hamiltonian.shape[1])), projected)


def split(a):
    high = a.astype(BF16)
    return high, (a - high.astype(F32)).astype(BF16)


def dot1(a, b, dims=NN):
    return lax.dot_general(a, b, dims, preferred_element_type=F32)


def dot3(a, b, dims=NN):
    ah, al = split(a)
    bh, bl = split(b)
    return dot1(ah, bh, dims) + (dot1(ah, bl, dims) + dot1(al, bh, dims))


def cut_call(product, basis, places):
    _, nvec = product.shape
    half = nvec // 2
    piece = 6 * half // 8
    tail = places.shape[0] - 1

    def body(places_ref, p_ref, b_ref, keep_ref, send_ref, buf):
        p = p_ref[...]
        own = places_ref[tail]
        pt_high, pt_low = split(p.T)
        bt = b_ref[...].astype(F32).T.astype(BF16)
        p_high, p_low = split(p)
        cross = dot1(pt_high, p_low)
        gram = dot1(pt_high, p_high) + (cross + dot1(pt_low, p_high))
        coupling = dot1(bt, p_high) + dot1(bt, p_low)
        coupling = 0.5 * (coupling + coupling.T)
        at = 0
        for a in (gram, coupling):
            for i, j in ((0, 0), (1, 0), (1, 1)):
                buf[at * half:(at + 1) * half, :] = a[i * half:(i + 1) * half, j * half:(j + 1) * half]
                at += 1
        for m in range(4):
            keep_ref[m] = buf[pl.ds(pl.multiple_of((own ^ m) * piece, 8), piece), :]
            send_ref[m] = buf[pl.ds(pl.multiple_of((own ^ (m + 4)) * piece, 8), piece), :]

    vmem = pl.BlockSpec(memory_space=pltpu.VMEM)
    shape = jax.ShapeDtypeStruct((4, piece, half), F32)
    return pl.pallas_call(
        body,
        name="cut_pieces",
        out_shape=(shape, shape),
        in_specs=[pl.BlockSpec(memory_space=pltpu.SMEM), vmem, vmem],
        out_specs=(vmem, vmem),
        scratch_shapes=[pltpu.VMEM((6 * half, half), F32)],
        compiler_params=pltpu.CompilerParams(vmem_limit_bytes=16 << 20),
    )(places, product, basis)


BUFFERS = 5


def stage_call(hamiltonian, units, near, places, offset, ready, ahead, acc):
    n = len(units)
    rows, _ = hamiltonian.shape
    width, nvec = units[0].shape
    first = acc is None
    count = 3 if near else 2

    def body(places_ref, h_ref, *rest):
        unit_refs, rest = rest[:n], rest[n:]
        if not first:
            sums, rest = rest[:count], rest[count:]
        totals, rest = rest[:count], rest[count:]
        ring, out_ref = totals[:2]
        ubuf, hsem, usem = rest

        def fetch(i):
            at = pl.multiple_of(places_ref[offset + i] * width, 128)
            slot = lax.rem(offset + i, BUFFERS)
            return pltpu.make_async_copy(h_ref.at[:, pl.ds(at, width)], ring.at[slot], hsem.at[slot])

        for i in range(n):
            if ready <= i < min(BUFFERS, n + ahead):
                fetch(i).start()
            pltpu.make_async_copy(unit_refs[i], ubuf.at[i], usem.at[i]).start()
        for i in range(n, min(BUFFERS, n + ahead)):
            fetch(i).start()
        for k in range(1, count):
            totals[k][...] = jnp.zeros_like(totals[k]) if first else sums[k][...]

        def step(i, correlate):
            pltpu.make_async_copy(ubuf.at[i], ubuf.at[i], usem.at[i]).wait()

            @pl.when(i >= ready)
            def _():
                fetch(i).wait()

            high, low = split(ring[lax.rem(offset + i, BUFFERS)])
            u = ubuf[i]
            if correlate:
                totals[2][...] += lax.dot_general(u, u, (((0,), (0,)), ((), ())), preferred_element_type=F32)
            out_ref[...] += dot1(high, u) + dot1(low, u)

            @pl.when(i + BUFFERS < n + ahead)
            def _():
                fetch(i + BUFFERS).start()

        def near_step(i, _):
            step(i, True)
            return 0

        def far_step(i, _):
            step(i, False)
            return 0

        if near:
            lax.fori_loop(0, near, near_step, 0)
        if near < n:
            lax.fori_loop(near, n, far_step, 0)
        for i in range(n, n + ahead):
            fetch(i).wait()

    any_spec = pl.BlockSpec(memory_space=pl.ANY)
    vmem = pl.BlockSpec(memory_space=pltpu.VMEM)
    operands = [places, hamiltonian, *units]
    in_specs = [pl.BlockSpec(memory_space=pltpu.SMEM), any_spec] + [any_spec] * n
    aliases = {}
    if not first:
        aliases = {len(operands) + k: k for k in range(count)}
        operands += list(acc[:count])
        in_specs += [vmem] * count
    return pl.pallas_call(
        body,
        name="stage_product",
        out_shape=(
            jax.ShapeDtypeStruct((BUFFERS, rows, width), F32),
            jax.ShapeDtypeStruct((rows, nvec), F32),
            jax.ShapeDtypeStruct((nvec, nvec), F32),
        )[:count],
        in_specs=in_specs,
        out_specs=(vmem,) * count,
        scratch_shapes=[
            pltpu.VMEM((n, width, nvec), BF16),
            pltpu.SemaphoreType.DMA((BUFFERS,)),
            pltpu.SemaphoreType.DMA((n,)),
        ],
        input_output_aliases=aliases,
        cost_estimate=pl.CostEstimate(
            flops=4 * n * rows * width * nvec, transcendentals=0, bytes_accessed=4 * n * rows * width
        ),
        compiler_params=pltpu.CompilerParams(vmem_limit_bytes=8 << 20),
    )(*operands)


def refine(a):
    n = a.shape[0]
    i = lax.broadcasted_iota(jnp.int32, (n, n), 0)
    j = lax.broadcasted_iota(jnp.int32, (n, n), 1)
    eye = jnp.where(i == j, 1.0, 0.0).astype(F32)
    weight = jnp.where(i > j, 1.0, jnp.where(i == j, 0.5, 0.0)).astype(F32)
    diagonal = jnp.where(i == j, a, 0.0)
    scale_row = lax.rsqrt(jnp.sum(diagonal, axis=0, keepdims=True))
    scale_col = lax.rsqrt(jnp.sum(diagonal, axis=1, keepdims=True))
    k = a * scale_row * scale_col
    e = k - eye
    x = (e * weight).astype(BF16)
    x = (e - dot1(x, x, NT)) * weight
    xh = x.astype(BF16)
    m = eye - x + dot1(xh, xh) * jnp.where(i >= j, 1.0, 0.0)

    def residual(m):
        return dot3(dot3(m, k), m, NT) - eye

    m = m - dot1((residual(m) * weight).astype(BF16), m.astype(BF16))
    e = residual(m)
    norm = jnp.max(jnp.sum(jnp.abs(e), axis=1))
    m = m - dot1((e * weight).astype(BF16), m.astype(BF16))
    return m * scale_row, norm


def eliminate(a, out_ref, work_a, work_w):
    n = a.shape[0]
    i = lax.broadcasted_iota(jnp.int32, (n, n), 0)
    j = lax.broadcasted_iota(jnp.int32, (n, n), 1)
    work_a[...] = a
    work_w[...] = jnp.where(i == j, 1.0, 0.0).astype(F32)
    lane = lax.broadcasted_iota(jnp.int32, (1, n), 1)
    row = lax.broadcasted_iota(jnp.int32, (n, 1), 0)

    def column(s, _):
        top = work_a[pl.ds(s, 1), :]
        top_w = work_w[pl.ds(s, 1), :]
        inverse = 1.0 / jnp.sum(jnp.where(lane == s, top, 0.0), axis=1, keepdims=True)
        at = work_a[...]
        col = jnp.sum(jnp.where(lane == s, at, 0.0), axis=1, keepdims=True)
        col = jnp.where(row > s, col * inverse, 0.0)
        work_a[...] = at - col * top
        work_w[...] = work_w[...] - col * top_w
        return 0

    lax.fori_loop(0, n, column, 0)
    pivots = jnp.sum(jnp.where(i == j, work_a[...], 0.0), axis=1, keepdims=True)
    out_ref[...] = work_w[...] * lax.rsqrt(pivots)


def inverse_factor(a_ref, out_ref, work_a, work_w):
    out_ref[...], norm = refine(a_ref[...])

    @pl.when(jnp.logical_not(norm < 3e-3))
    def _():
        eliminate(a_ref[...], out_ref, work_a, work_w)


def inverse_call(near, far):
    vmem = pl.BlockSpec(memory_space=pltpu.VMEM)
    square = pltpu.VMEM(near.shape, F32)

    def body(near_ref, far_ref, out_ref, whole, work_a, work_w):
        whole[...] = near_ref[...] + far_ref[...]
        inverse_factor(whole, out_ref, work_a, work_w)

    return pl.pallas_call(
        body,
        name="inverse_factor",
        out_shape=jax.ShapeDtypeStruct(near.shape, F32),
        in_specs=[vmem, vmem],
        out_specs=vmem,
        scratch_shapes=[square, square, square],
        cost_estimate=pl.CostEstimate(flops=60 * near.shape[0] ** 3, transcendentals=0, bytes_accessed=0),
        compiler_params=pltpu.CompilerParams(vmem_limit_bytes=12 << 20),
    )(near, far)


def finish_call(product, mine, other, low, places, scale):
    rows, nvec = product.shape
    half = nvec // 2
    _, piece, _ = mine.shape
    tail = places.shape[0] - 1

    def body(places_ref, p_ref, mine_ref, other_ref, low_ref, ritz_ref, projected_ref, pbuf, buf, whole, inv, work_a, work_w, sem):
        copy = pltpu.make_async_copy(p_ref, pbuf, sem)
        copy.start()
        own = places_ref[tail]
        for m in range(4):
            buf[pl.ds(pl.multiple_of((own ^ m) * piece, 8), piece), :] = mine_ref[m]
            buf[pl.ds(pl.multiple_of((own ^ (m + 4)) * piece, 8), piece), :] = other_ref[m]
        for q in range(2):
            at = 3 * q * half
            corner = buf[at + half:at + 2 * half, :]
            whole[q, :half, :half] = buf[at:at + half, :]
            whole[q, half:, :half] = corner
            whole[q, :half, half:] = corner.T
            whole[q, half:, half:] = buf[at + 2 * half:at + 3 * half, :]
        low = low_ref[...]
        projected_ref[...] = dot3(dot3(low, whole[1]), low, NT)
        inverse_factor(whole.at[0], inv, work_a, work_w)
        copy.wait()
        ritz_ref[...] = dot3(pbuf[...], inv[...] * scale, NT)

    vmem = pl.BlockSpec(memory_space=pltpu.VMEM)
    square = pltpu.VMEM((nvec, nvec), F32)
    return pl.pallas_call(
        body,
        name="finish",
        out_shape=(jax.ShapeDtypeStruct((rows, nvec), F32), jax.ShapeDtypeStruct((nvec, nvec), F32)),
        in_specs=[pl.BlockSpec(memory_space=pltpu.SMEM), pl.BlockSpec(memory_space=pl.ANY), vmem, vmem, vmem],
        out_specs=(vmem, vmem),
        scratch_shapes=[
            pltpu.VMEM((rows, nvec), F32),
            pltpu.VMEM((6 * half, half), F32),
            pltpu.VMEM((2, nvec, nvec), F32),
            square,
            square,
            square,
            pltpu.SemaphoreType.DMA,
        ],
        compiler_params=pltpu.CompilerParams(vmem_limit_bytes=16 << 20),
    )(places, product, mine, other, low)


STAGES = (
    ((4, 0, 4), (1, 0, 1), (2, 0, 2)),
    ((5, 4, 1), (6, 4, 2), (8, 0, 8), (3, 2, 1)),
    ((7, 5, 2),),
    ((12, 8, 4), (9, 8, 1), (10, 8, 2)),
    ((14, 12, 2), (13, 9, 4), (11, 10, 1)),
    ((15, 14, 1),),
)
TURNS = (
    ((0,), (0,), 2, (4, 1, 2)),
    ((4, 1, 2), (), 1, (5, 6, 8, 3)),
    ((5, 6), (4, 1, 2), 1, (7, 8, 3)),
    ((8, 3, 7), (5, 6), 1, (12, 9, 10)),
    ((12, 9, 10), (8, 3, 7), 1, (14, 13, 11)),
    ((14, 13, 11), (12, 9, 10), 1, (15,)),
    ((15,), (14, 13, 11), 1, ()),
    ((), (15,), 0, ()),
)


def shards_pairs(hamiltonian, vectors):
    chips = lax.axis_size("rows")
    here = lax.axis_index("rows")
    core = lax.axis_index("chip")

    def from_chip(a, m):
        return lax.ppermute(a, "rows", [(s, s ^ m) for s in range(chips)])

    def from_core(a):
        return lax.ppermute(a, "chip", [(0, 1), (1, 0)])

    basis = vectors.astype(BF16)
    order = [2 * m + far for turn in TURNS for far in range(2) for m in turn[far]]
    places = jnp.concatenate(
        [(2 * here + core) ^ jnp.array(order, jnp.int32), (4 * core + here % 4).astype(jnp.int32).reshape(1)]
    )
    mine = {0: basis}
    acc = None
    other = {}
    offset = ready = 0
    for stage in STAGES:
        for m, source, step in stage:
            mine[m] = from_chip(mine[source], step)
    for t, (near, far, ahead, _) in enumerate(TURNS):
        for m in near:
            other[m] = from_core(mine[m])
        units = [mine[m] for m in near] + [other[m] for m in far]
        sums = stage_call(hamiltonian, units, len(near), places, offset, ready, ahead, acc)
        acc = sums if near else (*sums, acc[2])
        offset += len(units)
        ready = ahead
        if near:
            correlation = acc[2]
        if t == len(TURNS) - 2:
            correlation_far = from_core(correlation)
    product = acc[1]
    keep, send = cut_call(product, basis, places)
    a = keep + from_core(send)
    b = a[0] + from_chip(a[1], 1) + from_chip(a[2], 2) + from_chip(a[3], 3)
    b = b + from_chip(b, 4) + from_chip(b, 8) + from_chip(b, 12)
    mine4 = jnp.stack([b, from_chip(b, 1), from_chip(b, 2), from_chip(b, 3)])
    other4 = from_core(mine4)
    low = inverse_call(correlation, correlation_far)
    return finish_call(product, mine4, other4, low, places, float(hamiltonian.shape[1]) ** 0.5)


def solution(mesh):
    in_specs = (P(AXES, None), P(AXES, None))
    out_specs = (P(AXES, None), P())
    pairs = mesh.shape["rows"] == 16 and mesh.shape["chip"] == 2
    body = shards_pairs if pairs else shards_plain
    return jax.shard_map(body, mesh=mesh, in_specs=in_specs, out_specs=out_specs, check_vma=False)
```

```python
import jax
import jax.numpy as jnp
from jax import lax
from jax.experimental import pallas as pl
from jax.experimental.pallas import tpu as pltpu
from jax.sharding import PartitionSpec as P


AXES = ("rows", "chip")
F32 = jnp.float32
BF16 = jnp.bfloat16
NN = (((1,), (0,)), ((), ()))
NT = (((1,), (1,)), ((), ()))


def shards_plain(hamiltonian, vectors):
    highest = lax.Precision.HIGHEST
    basis = vectors.astype(BF16)
    widened = basis.astype(F32)
    correlation_part = jnp.dot(basis.T, basis, preferred_element_type=F32)
    whole = lax.all_gather(basis, AXES, axis=0, tiled=True)
    product = jnp.dot(hamiltonian, whole.astype(F32), precision=highest)
    coupling_part = jnp.dot(widened.T, product, precision=highest)
    gram_part = jnp.dot(product.T, product, precision=highest)
    correlation, coupling, gram = lax.psum((correlation_part, coupling_part, gram_part), AXES)
    symmetric = 0.5 * (coupling + coupling.T)
    lower = jnp.linalg.cholesky(correlation)
    half = lax.linalg.triangular_solve(lower, symmetric, left_side=True, lower=True)
    projected = lax.linalg.triangular_solve(lower, half.T, left_side=True, lower=True)
    factor = jnp.linalg.cholesky(gram)
    rotated = lax.linalg.triangular_solve(factor, product.T, left_side=True, lower=True)
    return (rotated.T * jnp.sqrt(F32(hamiltonian.shape[1])), projected)


def split(a):
    high = a.astype(BF16)
    return high, (a - high.astype(F32)).astype(BF16)


def dot1(a, b, dims=NN):
    return lax.dot_general(a, b, dims, preferred_element_type=F32)


def dot3(a, b, dims=NN):
    ah, al = split(a)
    bh, bl = split(b)
    return dot1(ah, bh, dims) + (dot1(ah, bl, dims) + dot1(al, bh, dims))


def cut_call(product, basis, places):
    _, nvec = product.shape
    half = nvec // 2
    piece = 6 * half // 8
    tail = places.shape[0] - 1

    def body(places_ref, p_ref, b_ref, keep_ref, send_ref, buf):
        p = p_ref[...]
        own = places_ref[tail]
        pt_high, pt_low = split(p.T)
        bt = b_ref[...].astype(F32).T.astype(BF16)
        p_high, p_low = split(p)
        cross = dot1(pt_high, p_low)
        gram = dot1(pt_high, p_high) + (cross + dot1(pt_low, p_high))
        coupling = dot1(bt, p_high) + dot1(bt, p_low)
        coupling = 0.5 * (coupling + coupling.T)
        at = 0
        for a in (gram, coupling):
            for i, j in ((0, 0), (1, 0), (1, 1)):
                buf[at * half:(at + 1) * half, :] = a[i * half:(i + 1) * half, j * half:(j + 1) * half]
                at += 1
        for m in range(4):
            keep_ref[m] = buf[pl.ds(pl.multiple_of((own ^ m) * piece, 8), piece), :]
            send_ref[m] = buf[pl.ds(pl.multiple_of((own ^ (m + 4)) * piece, 8), piece), :]

    vmem = pl.BlockSpec(memory_space=pltpu.VMEM)
    shape = jax.ShapeDtypeStruct((4, piece, half), F32)
    return pl.pallas_call(
        body,
        name="cut_pieces",
        out_shape=(shape, shape),
        in_specs=[pl.BlockSpec(memory_space=pltpu.SMEM), vmem, vmem],
        out_specs=(vmem, vmem),
        scratch_shapes=[pltpu.VMEM((6 * half, half), F32)],
        compiler_params=pltpu.CompilerParams(vmem_limit_bytes=16 << 20),
    )(places, product, basis)


BUFFERS = 6


def stage_call(hamiltonian, units, near, places, offset, ready, ahead, acc):
    n = len(units)
    rows, _ = hamiltonian.shape
    width, nvec = units[0].shape
    first = acc is None
    count = 3 if near else 2

    def body(places_ref, h_ref, *rest):
        unit_refs, rest = rest[:n], rest[n:]
        if not first:
            sums, rest = rest[:count], rest[count:]
        totals, rest = rest[:count], rest[count:]
        ring, out_ref = totals[:2]
        ubuf, hsem, usem = rest

        def fetch(i):
            at = pl.multiple_of(places_ref[offset + i] * width, 128)
            slot = lax.rem(offset + i, BUFFERS)
            return pltpu.make_async_copy(h_ref.at[:, pl.ds(at, width)], ring.at[slot], hsem.at[slot])

        for i in range(n):
            if ready <= i < min(BUFFERS, n + ahead):
                fetch(i).start()
            pltpu.make_async_copy(unit_refs[i], ubuf.at[i], usem.at[i]).start()
        for i in range(n, min(BUFFERS, n + ahead)):
            fetch(i).start()
        for k in range(1, count):
            totals[k][...] = jnp.zeros_like(totals[k]) if first else sums[k][...]

        def step(i, correlate):
            pltpu.make_async_copy(ubuf.at[i], ubuf.at[i], usem.at[i]).wait()

            @pl.when(i >= ready)
            def _():
                fetch(i).wait()

            high, low = split(ring[lax.rem(offset + i, BUFFERS)])
            u = ubuf[i]
            if correlate:
                totals[2][...] += lax.dot_general(u, u, (((0,), (0,)), ((), ())), preferred_element_type=F32)
            out_ref[...] += dot1(high, u) + dot1(low, u)

            @pl.when(i + BUFFERS < n + ahead)
            def _():
                fetch(i + BUFFERS).start()

        def near_step(i, _):
            step(i, True)
            return 0

        def far_step(i, _):
            step(i, False)
            return 0

        if near:
            lax.fori_loop(0, near, near_step, 0)
        if near < n:
            lax.fori_loop(near, n, far_step, 0)
        for i in range(n, n + ahead):
            fetch(i).wait()

    any_spec = pl.BlockSpec(memory_space=pl.ANY)
    vmem = pl.BlockSpec(memory_space=pltpu.VMEM)
    operands = [places, hamiltonian, *units]
    in_specs = [pl.BlockSpec(memory_space=pltpu.SMEM), any_spec] + [any_spec] * n
    aliases = {}
    if not first:
        aliases = {len(operands) + k: k for k in range(count)}
        operands += list(acc[:count])
        in_specs += [vmem] * count
    return pl.pallas_call(
        body,
        name="stage_product",
        out_shape=(
            jax.ShapeDtypeStruct((BUFFERS, rows, width), F32),
            jax.ShapeDtypeStruct((rows, nvec), F32),
            jax.ShapeDtypeStruct((nvec, nvec), F32),
        )[:count],
        in_specs=in_specs,
        out_specs=(vmem,) * count,
        scratch_shapes=[
            pltpu.VMEM((n, width, nvec), BF16),
            pltpu.SemaphoreType.DMA((BUFFERS,)),
            pltpu.SemaphoreType.DMA((n,)),
        ],
        input_output_aliases=aliases,
        cost_estimate=pl.CostEstimate(
            flops=4 * n * rows * width * nvec, transcendentals=0, bytes_accessed=4 * n * rows * width
        ),
        compiler_params=pltpu.CompilerParams(vmem_limit_bytes=8 << 20),
    )(*operands)


def refine(a):
    n = a.shape[0]
    i = lax.broadcasted_iota(jnp.int32, (n, n), 0)
    j = lax.broadcasted_iota(jnp.int32, (n, n), 1)
    eye = jnp.where(i == j, 1.0, 0.0).astype(F32)
    weight = jnp.where(i > j, 1.0, jnp.where(i == j, 0.5, 0.0)).astype(F32)
    diagonal = jnp.where(i == j, a, 0.0)
    scale_row = lax.rsqrt(jnp.sum(diagonal, axis=0, keepdims=True))
    scale_col = lax.rsqrt(jnp.sum(diagonal, axis=1, keepdims=True))
    k = a * scale_row * scale_col
    e = k - eye
    x = (e * weight).astype(BF16)
    x = (e - dot1(x, x, NT)) * weight
    xh = x.astype(BF16)
    m = eye - x + dot1(xh, xh) * jnp.where(i >= j, 1.0, 0.0)

    def residual(m):
        return dot3(dot3(m, k), m, NT) - eye

    m = m - dot1((residual(m) * weight).astype(BF16), m.astype(BF16))
    e = residual(m)
    norm = jnp.max(jnp.sum(jnp.abs(e), axis=1))
    m = m - dot1((e * weight).astype(BF16), m.astype(BF16))
    return m * scale_row, norm


def eliminate(a, out_ref, work_a, work_w):
    n = a.shape[0]
    i = lax.broadcasted_iota(jnp.int32, (n, n), 0)
    j = lax.broadcasted_iota(jnp.int32, (n, n), 1)
    work_a[...] = a
    work_w[...] = jnp.where(i == j, 1.0, 0.0).astype(F32)
    lane = lax.broadcasted_iota(jnp.int32, (1, n), 1)
    row = lax.broadcasted_iota(jnp.int32, (n, 1), 0)

    def column(s, _):
        top = work_a[pl.ds(s, 1), :]
        top_w = work_w[pl.ds(s, 1), :]
        inverse = 1.0 / jnp.sum(jnp.where(lane == s, top, 0.0), axis=1, keepdims=True)
        at = work_a[...]
        col = jnp.sum(jnp.where(lane == s, at, 0.0), axis=1, keepdims=True)
        col = jnp.where(row > s, col * inverse, 0.0)
        work_a[...] = at - col * top
        work_w[...] = work_w[...] - col * top_w
        return 0

    lax.fori_loop(0, n, column, 0)
    pivots = jnp.sum(jnp.where(i == j, work_a[...], 0.0), axis=1, keepdims=True)
    out_ref[...] = work_w[...] * lax.rsqrt(pivots)


def inverse_factor(a_ref, out_ref, work_a, work_w):
    out_ref[...], norm = refine(a_ref[...])

    @pl.when(jnp.logical_not(norm < 3e-3))
    def _():
        eliminate(a_ref[...], out_ref, work_a, work_w)


def inverse_call(near, far):
    vmem = pl.BlockSpec(memory_space=pltpu.VMEM)
    square = pltpu.VMEM(near.shape, F32)

    def body(near_ref, far_ref, out_ref, whole, work_a, work_w):
        whole[...] = near_ref[...] + far_ref[...]
        inverse_factor(whole, out_ref, work_a, work_w)

    return pl.pallas_call(
        body,
        name="inverse_factor",
        out_shape=jax.ShapeDtypeStruct(near.shape, F32),
        in_specs=[vmem, vmem],
        out_specs=vmem,
        scratch_shapes=[square, square, square],
        cost_estimate=pl.CostEstimate(flops=60 * near.shape[0] ** 3, transcendentals=0, bytes_accessed=0),
        compiler_params=pltpu.CompilerParams(vmem_limit_bytes=12 << 20),
    )(near, far)


def finish_call(product, mine, other, low, places, scale):
    rows, nvec = product.shape
    half = nvec // 2
    _, piece, _ = mine.shape
    tail = places.shape[0] - 1

    def body(places_ref, p_ref, mine_ref, other_ref, low_ref, ritz_ref, projected_ref, pbuf, buf, whole, inv, work_a, work_w, sem):
        copy = pltpu.make_async_copy(p_ref, pbuf, sem)
        copy.start()
        own = places_ref[tail]
        for m in range(4):
            buf[pl.ds(pl.multiple_of((own ^ m) * piece, 8), piece), :] = mine_ref[m]
            buf[pl.ds(pl.multiple_of((own ^ (m + 4)) * piece, 8), piece), :] = other_ref[m]
        for q in range(2):
            at = 3 * q * half
            corner = buf[at + half:at + 2 * half, :]
            whole[q, :half, :half] = buf[at:at + half, :]
            whole[q, half:, :half] = corner
            whole[q, :half, half:] = corner.T
            whole[q, half:, half:] = buf[at + 2 * half:at + 3 * half, :]
        low = low_ref[...]
        projected_ref[...] = dot3(dot3(low, whole[1]), low, NT)
        inverse_factor(whole.at[0], inv, work_a, work_w)
        copy.wait()
        ritz_ref[...] = dot3(pbuf[...], inv[...] * scale, NT)

    vmem = pl.BlockSpec(memory_space=pltpu.VMEM)
    square = pltpu.VMEM((nvec, nvec), F32)
    return pl.pallas_call(
        body,
        name="finish",
        out_shape=(jax.ShapeDtypeStruct((rows, nvec), F32), jax.ShapeDtypeStruct((nvec, nvec), F32)),
        in_specs=[pl.BlockSpec(memory_space=pltpu.SMEM), pl.BlockSpec(memory_space=pl.ANY), vmem, vmem, vmem],
        out_specs=(vmem, vmem),
        scratch_shapes=[
            pltpu.VMEM((rows, nvec), F32),
            pltpu.VMEM((6 * half, half), F32),
            pltpu.VMEM((2, nvec, nvec), F32),
            square,
            square,
            square,
            pltpu.SemaphoreType.DMA,
        ],
        compiler_params=pltpu.CompilerParams(vmem_limit_bytes=16 << 20),
    )(places, product, mine, other, low)


STAGES = (
    ((4, 0, 4), (1, 0, 1), (2, 0, 2)),
    ((5, 4, 1), (6, 4, 2), (8, 0, 8), (3, 2, 1)),
    ((7, 5, 2),),
    ((12, 8, 4), (9, 8, 1), (10, 8, 2)),
    ((14, 12, 2), (13, 9, 4), (11, 10, 1)),
    ((15, 14, 1),),
)
TURNS = (
    ((0,), (0,), 2, (4, 1, 2)),
    ((4, 1, 2), (), 1, (5, 6, 8, 3)),
    ((5, 6), (4, 1, 2), 1, (7, 8, 3)),
    ((8, 3, 7), (5, 6), 1, (12, 9, 10)),
    ((12, 9, 10), (8, 3, 7), 1, (14, 13, 11)),
    ((14, 13, 11), (12, 9, 10), 1, (15,)),
    ((15,), (14, 13, 11), 1, ()),
    ((), (15,), 0, ()),
)


def shards_pairs(hamiltonian, vectors):
    chips = lax.axis_size("rows")
    here = lax.axis_index("rows")
    core = lax.axis_index("chip")

    def from_chip(a, m):
        return lax.ppermute(a, "rows", [(s, s ^ m) for s in range(chips)])

    def from_core(a):
        return lax.ppermute(a, "chip", [(0, 1), (1, 0)])

    basis = vectors.astype(BF16)
    order = [2 * m + far for turn in TURNS for far in range(2) for m in turn[far]]
    places = jnp.concatenate(
        [(2 * here + core) ^ jnp.array(order, jnp.int32), (4 * core + here % 4).astype(jnp.int32).reshape(1)]
    )
    mine = {0: basis}
    acc = None
    other = {}
    offset = ready = 0
    for stage in STAGES:
        for m, source, step in stage:
            mine[m] = from_chip(mine[source], step)
    for t, (near, far, ahead, _) in enumerate(TURNS):
        for m in near:
            other[m] = from_core(mine[m])
        units = [mine[m] for m in near] + [other[m] for m in far]
        sums = stage_call(hamiltonian, units, len(near), places, offset, ready, ahead, acc)
        acc = sums if near else (*sums, acc[2])
        offset += len(units)
        ready = ahead
        if near:
            correlation = acc[2]
        if t == len(TURNS) - 2:
            correlation_far = from_core(correlation)
    product = acc[1]
    keep, send = cut_call(product, basis, places)
    a = keep + from_core(send)

    def from_three(arrays, steps):
        got = {}
        for a, step in zip(arrays, steps):
            got[step] = from_chip(a, step)
        return [got[step] for step in sorted(steps)]

    x, y, xy = from_three((a[3], a[2], a[1]), (3, 2, 1))
    b = a[0] + x + y + xy
    z = from_three((b, b, b), (12, 8, 4))
    b = b + z[0] + z[1] + z[2]
    mine4 = jnp.stack([b, *from_three((b, b, b), (3, 2, 1))])
    other4 = from_core(mine4)
    low = inverse_call(correlation, correlation_far)
    return finish_call(product, mine4, other4, low, places, float(hamiltonian.shape[1]) ** 0.5)


def solution(mesh):
    in_specs = (P(AXES, None), P(AXES, None))
    out_specs = (P(AXES, None), P())
    pairs = mesh.shape["rows"] == 16 and mesh.shape["chip"] == 2
    body = shards_pairs if pairs else shards_plain
    return jax.shard_map(body, mesh=mesh, in_specs=in_specs, out_specs=out_specs, check_vma=False)
```
